512 devices in a mesh: seq: 32 (over y_lo, z), head: 16 (over x, y_hi, core).
Axes of the slice: x: 4, y: 4 (y_hi: 2, y_lo: 2; y = y_hi * 2 + y_lo), z: 16, core: 2. Of those that a mesh axis runs over, the one named last changes fastest.
Arguments:
- queries: bfloat16 [4096, 8192], P('seq', 'head'), may hold values from -6 to 6
- vision: bfloat16 [6400, 8192], P('seq'), may hold values from -6 to 6
- kv_weight: bfloat16 [2, 8192, 1024], P(None, None, 'head'), may hold values from -0.75 to 0.75
- out_weight: bfloat16 [8192, 8192], P('head', 'seq'), may hold values from -0.125 to 0.125
- q_gain: float32 [128], replicated, may hold values from 0.1 to 1.9
- k_gain: float32 [128], replicated, may hold values from 0.1 to 1.9
- tile_counts: int32 [4], replicated, may hold values from 800 to 1600, as said below
- spans: int32 [4096, 2], P('seq'), may hold values from 0 to 4, as said below
Outputs:
- output: bfloat16 [4096, 8192], P('seq', 'head')
The draws below stay inside these ranges and needn't reach their ends.
Inputs may be any that keep to these rules, and one draw needn't show every extreme that they name: `tile_counts`: every tile holds at least 800 vision tokens in its first slots; one tile is full with exactly 1600. For every token spans[t, 0] < spans[t, 1], so each token attends one or more whole tiles.
All inputs are finite; a program needn't handle non-finite values.
Results may differ from the reference program's by a relative error of at most 0.0085.
Values may be sent and summed in bfloat16 or wider, within the bound.
No kernel may reach another device: no remote copies, remote signals or barrier semaphores. Data moves between devices by JAX's collectives and lax.ppermute only.
A program may use at most 64 MiB of HBM per device.

```python
import math
import jax
import jax.numpy as jnp
from jax import lax

D = 8192
HD = 128
GROUP = 8
TILES = 4
QH = 64
KV_HEADS = 8
TEXT = 4096
VIS = 6400
CAP = 1600


def draw_tile_counts(key, part):
    counts = jax.random.randint(jax.random.fold_in(key, 11), (TILES,), CAP // 2, CAP + 1)
    chosen_tile = jax.random.randint(jax.random.fold_in(key, 12), (), 0, TILES)
    return jnp.where(jnp.arange(TILES) == chosen_tile, CAP, counts).astype(jnp.int32)


def draw_spans(key, part):
    first_tile = jax.random.randint(jax.random.fold_in(key, 21), (TEXT,), 0, TILES)
    tile_span = jax.random.randint(jax.random.fold_in(key, 22), (TEXT,), 1, TILES + 1)
    end_tile = jnp.minimum(first_tile + tile_span, TILES)
    lead_row = jnp.arange(TEXT) == 0
    first_tile = jnp.where(lead_row, 0, first_tile)
    end_tile = jnp.where(lead_row, TILES, end_tile)
    return jnp.stack([first_tile, end_tile], axis=1).astype(jnp.int32)


def with_spikes(entries, rng, source, target, blocks, factor):
    owner, partner = [(jnp.arange(entries.shape[position]) // (entries.shape[position] // blocks)).reshape([-1 if axis == position else 1 for axis in range(entries.ndim)]) for position in (source, target)]
    chosen = jax.random.permutation(rng, blocks)[partner]
    strong = (owner == chosen) | (owner == (partner + blocks // 2) % blocks)
    return jnp.where(strong, factor * entries, entries)


def block_levels(stream_key, dims, split, smallest, high):
    def one(position, blocks):
        steps = jax.random.uniform(jax.random.fold_in(jax.random.fold_in(stream_key, 6), position), (blocks,), jnp.float32, smallest / len(split), high / len(split))
        return jnp.repeat(jnp.exp(steps), dims[position] // blocks).reshape((-1,) + (1,) * (len(dims) - position - 1))

    loudness = one(*split[0])
    for cut in split[1:]:
        loudness = loudness * one(*cut)
    return loudness


def bell_draw(key, dims, width, most, shards=(), kind=jnp.bfloat16):
    result = width * jax.random.normal(key, dims, jnp.float32)
    if shards:
        result = result * block_levels(key, dims, shards, -0.22, 0.18)
    return jnp.clip(result, -most, most).astype(kind)


def heavy_noise(stream_key, dims, deviation, reach, cuts, heavy, held_as=jnp.bfloat16):
    array = deviation * jax.random.normal(stream_key, dims, jnp.float32)
    if cuts:
        array = array * block_levels(stream_key, dims, cuts, -0.22, 0.18)
    return jnp.clip(with_spikes(array, jax.random.fold_in(stream_key, 3), *heavy), -reach, reach).astype(held_as)


def setup_inputs(seed: int = 0) -> dict:
    streams_of = jax.random.split(jax.random.key(seed), 9)
    return {
        "queries": bell_draw(streams_of[0], (TEXT, QH * HD), 1.0, 6.0, ((0, 32), (1, 16))),
        "vision": bell_draw(streams_of[1], (VIS, D), 1.0, 6.0, ((0, 32),)),
        "kv_weight": bell_draw(streams_of[2], (2, D, KV_HEADS * HD), (HD // 2) ** -0.5, 0.75, ((2, 16),)),
        "out_weight": heavy_noise(streams_of[3], (QH * HD, D), (QH * HD) ** -0.5, 0.125, ((0, 16), (1, 32)), (0, 1, 32, 2.75)),
        "q_gain": jnp.clip(1.0 + 0.18 * jax.random.normal(streams_of[4], (HD,), jnp.float32), 0.1, 1.9),
        "k_gain": jnp.clip(1.0 + 0.18 * jax.random.normal(streams_of[5], (HD,), jnp.float32), 0.1, 1.9),
        "tile_counts": draw_tile_counts(jax.random.fold_in(streams_of[8], 71), 0),
        "spans": draw_spans(jax.random.fold_in(streams_of[8], 71), 0),
    }


EPSILON = 1e-05

def rms_scale(field, gain):
    mean_sq = lax.optimization_barrier(jnp.mean(field * field, axis=-1, keepdims=True))
    return field / jnp.sqrt(mean_sq + EPSILON) * gain

def reference(queries, vision, kv_weight, out_weight, q_gain, k_gain, tile_counts, spans):
    query_f = queries.astype(jnp.float32).reshape(TEXT, QH, HD)
    q_normed = rms_scale(query_f, q_gain).astype(jnp.bfloat16)
    key_raw = jnp.dot(vision, kv_weight[0], preferred_element_type=jnp.float32).reshape(VIS, KV_HEADS, HD)
    keys = rms_scale(key_raw, k_gain).astype(jnp.bfloat16)
    values = jnp.dot(vision, kv_weight[1], preferred_element_type=jnp.float32).astype(jnp.bfloat16).reshape(VIS, KV_HEADS, HD)
    key_index = jnp.arange(VIS, dtype=jnp.int32)
    tile_of = key_index // CAP
    slot_of = key_index % CAP
    present = slot_of < tile_counts[tile_of]
    allowed = present[None, :] & (spans[:, 0:1] <= tile_of[None, :]) & (tile_of[None, :] < spans[:, 1:2])
    q_heads = jnp.transpose(q_normed, (1, 0, 2))
    k_heads = jnp.transpose(keys, (1, 0, 2))
    v_heads = jnp.transpose(values, (1, 0, 2))
    factor = 1.0 / math.sqrt(HD)

    def one_head(head_index):
        group_index = head_index // GROUP
        scores = jnp.dot(q_heads[head_index], k_heads[group_index].T, preferred_element_type=jnp.float32) * factor
        weights = jnp.where(allowed, jnp.exp(scores), jnp.zeros_like(scores))
        totals = lax.optimization_barrier(jnp.sum(weights, axis=1))
        numer = jnp.dot(weights.astype(jnp.bfloat16), v_heads[group_index], preferred_element_type=jnp.float32)
        return (numer / totals[:, None]).astype(jnp.bfloat16)
    attended = lax.map(one_head, jnp.arange(QH, dtype=jnp.int32))
    attended = jnp.transpose(attended, (1, 0, 2)).reshape(TEXT, QH * HD)
    return jnp.dot(attended, out_weight, preferred_element_type=jnp.float32).astype(jnp.bfloat16)
```

```python
import math

import jax
import jax.numpy as jnp
from jax import lax
from jax.experimental import pallas as pl
from jax.experimental.pallas import tpu as pltpu
from jax.sharding import Mesh, PartitionSpec as P

HD = 128
TILES = 4
EPSILON = 1e-05
NEG = -1e30
AXES = ("ylo", "z", "x", "yhi", "core")
SIZES = (2, 16, 4, 2, 2)
ROWS = 128
HEADS = 8
LOCAL = 200
TAKE = 112
SHIFT = LOCAL - TAKE
SLOTS = 16 * TAKE
BF = jnp.bfloat16
F32 = jnp.float32


def flat(ylo, z, x, yhi, core):
    return (((ylo * 16 + z) * 4 + x) * 2 + yhi) * 2 + core


def swapped(value, axis):
    return lax.ppermute(value, axis, [(0, 1), (1, 0)])


def moved(value, cross):
    pairs = []
    for ylo in range(2):
        for z in range(16):
            for x in range(4):
                for yhi in range(2):
                    for core in range(2):
                        target = flat(x // 2, z, 2 * ylo + x % 2, yhi, core ^ cross)
                        pairs.append((flat(ylo, z, x, yhi, core), target))
    return lax.ppermute(value, AXES, pairs)


def rms_scale(field, gain):
    mean_sq = jnp.mean(field * field, axis=-1, keepdims=True)
    return field / jnp.sqrt(mean_sq + EPSILON) * gain


def attend_kernel(core_ref, q_ref, qx_ref, kv_ref, kx_ref, numer_ref, total_ref, key_s, value_s):
    step = pl.program_id(0)

    @pl.when(step == 0)
    def _():
        for z in range(16):
            rows = pl.ds(z * TAKE, TAKE)
            key_s[rows, :HD] = kv_ref[z, :TAKE]
            value_s[rows, :HD] = kv_ref[z, TAKE:]
        key_s[:, HD:] = kx_ref[...]
        value_s[:, HD:] = jnp.ones((SLOTS, HD), BF)
        total_ref[...] = jnp.zeros_like(total_ref)

    query = jnp.concatenate([q_ref[...], qx_ref[...]], axis=1)
    scores = lax.dot_general(
        query, key_s[...], (((1,), (1,)), ((), ())), preferred_element_type=F32
    )
    weights = jnp.exp2(scores * (math.log2(math.e) / math.sqrt(HD))).astype(BF)
    result = jnp.dot(weights, value_s[...], preferred_element_type=F32)
    numer_ref[...] = result[:, :HD]
    head = (step + 4 * core_ref[0]) % HEADS
    lane = lax.broadcasted_iota(jnp.int32, (2 * ROWS, HD), 1)
    total_ref[...] += jnp.where(lane == head, result[:, HD:], 0.0)


def attend(core, query, query_ext, gathered, key_ext):
    whole = lambda *dims: pl.BlockSpec(dims, lambda h, c: (0,) * len(dims))
    return pl.pallas_call(
        attend_kernel,
        grid_spec=pltpu.PrefetchScalarGridSpec(
            num_scalar_prefetch=1,
            grid=(HEADS,),
            in_specs=[
                pl.BlockSpec((2 * ROWS, HD), lambda h, c: (0, h)),
                whole(2 * ROWS, HD),
                whole(16, 2 * TAKE, HD),
                whole(SLOTS, HD),
            ],
            out_specs=[
                pl.BlockSpec((2 * ROWS, HD), lambda h, c: (0, (h + 4 * c[0]) % HEADS)),
                whole(2 * ROWS, HD),
            ],
            scratch_shapes=[
                pltpu.VMEM((SLOTS, 2 * HD), BF),
                pltpu.VMEM((SLOTS, 2 * HD), BF),
            ],
        ),
        out_shape=[
            jax.ShapeDtypeStruct((2 * ROWS, HEADS * HD), F32),
            jax.ShapeDtypeStruct((2 * ROWS, HD), F32),
        ],
        compiler_params=pltpu.CompilerParams(
            dimension_semantics=("arbitrary",), vmem_limit_bytes=48 << 20
        ),
        name="attend",
    )(core, query, query_ext, gathered, key_ext)


def project_kernel(a_ref, w_ref, o_ref):
    weight = jnp.concatenate([w_ref[0], w_ref[1]], axis=1)
    result = jnp.dot(a_ref[...], weight, preferred_element_type=F32).astype(BF)
    o_ref[0, 0] = result[:ROWS]
    o_ref[1, 0] = result[ROWS:]


def project(attended, weight):
    depth = HEADS * HD
    return pl.pallas_call(
        project_kernel,
        grid=(8,),
        in_specs=[
            pl.BlockSpec((2 * ROWS, depth), lambda j: (0, 0)),
            pl.BlockSpec((2, depth, 128), lambda j: (j, 0, 0)),
        ],
        out_specs=pl.BlockSpec((2, 1, ROWS, 256), lambda j: (0, j, 0, 0)),
        out_shape=jax.ShapeDtypeStruct((2, 8, ROWS, 256), BF),
        compiler_params=pltpu.CompilerParams(
            dimension_semantics=("arbitrary",), vmem_limit_bytes=48 << 20
        ),
        name="project",
    )(attended, weight)


def local(queries, vision, kv_weight, out_weight, q_gain, k_gain, tile_counts, spans):
    core = lax.axis_index("core")
    ylo = lax.axis_index("ylo")
    first = core == 0

    kept = lax.dynamic_slice_in_dim(out_weight, core * 128, 128, axis=1)
    sent = lax.dynamic_slice_in_dim(out_weight, (1 - core) * 128, 128, axis=1)
    got = swapped(sent, "core")
    upper = jnp.where(first, kept, got)
    lower = jnp.where(first, got, kept)
    weight = lax.all_gather(jnp.concatenate([upper, lower], axis=0), "z", axis=0, tiled=False)

    both = jnp.concatenate([kv_weight[0], kv_weight[1]], axis=1)
    projected = jnp.dot(vision, both, preferred_element_type=F32)
    mine = lax.dynamic_slice_in_dim(projected, core * SHIFT, TAKE, axis=0)
    theirs = swapped(lax.dynamic_slice_in_dim(projected, (1 - core) * SHIFT, TAKE, axis=0), "core")
    half = HD // 2
    left = jnp.where(first, mine, theirs)
    right = jnp.where(first, theirs, mine)
    key = rms_scale(jnp.concatenate([left[:, :half], right[:, :half]], axis=1), k_gain)
    value = jnp.concatenate([left[:, half:], right[:, half:]], axis=1)
    pair = jnp.concatenate([key, value], axis=0).astype(BF)
    gathered = lax.all_gather(pair, "z", axis=0, tiled=False)

    query_f = queries.astype(F32).reshape(ROWS, 4, HD)
    normed = rms_scale(query_f, q_gain).astype(BF).reshape(ROWS, 4 * HD)
    wide = jnp.concatenate([normed, swapped(normed, "core")], axis=1)
    other = swapped(wide, "ylo")
    other_spans = swapped(spans, "ylo")
    below = ylo == 0
    query = jnp.where(
        below, jnp.concatenate([wide, other], axis=0), jnp.concatenate([other, wide], axis=0)
    )
    span = jnp.where(
        below,
        jnp.concatenate([spans, other_spans], axis=0),
        jnp.concatenate([other_spans, spans], axis=0),
    )

    lane = jnp.arange(HD, dtype=jnp.int32)[None, :]
    inside = (span[:, :1] <= lane) & (lane < span[:, 1:])
    query_ext = jnp.where((lane <= TILES) & ~inside, NEG, 0.0).astype(BF)
    row = jnp.arange(SLOTS, dtype=jnp.int32)[:, None]
    block, item = row // TAKE, row % TAKE
    tile = 2 * ylo + block // 8
    slot = (block % 8) * LOCAL + core * SHIFT + item
    count = jnp.sum(jnp.where(tile == jnp.arange(TILES)[None, :], tile_counts[None, :], 0), axis=1)
    absent = (slot >= count[:, None]) | ((core == 1) & (item < 2 * TAKE - LOCAL))
    key_ext = jnp.where((lane == tile) | ((lane == TILES) & absent), 1.0, 0.0).astype(BF)

    numer, total = attend(
        jnp.reshape(core, (1,)).astype(jnp.int32), query, query_ext, gathered, key_ext
    )

    numer = numer + swapped(numer, "core")
    total = total + swapped(total, "core")
    high = lax.reduce_precision(total, 8, 7)
    low = jnp.concatenate([jnp.zeros((2 * ROWS, 8), F32), (total - high)[:, : HD - 8]], axis=1)
    payload = jnp.concatenate([numer, high + low], axis=1).astype(BF)
    rest = swapped(payload, "ylo").astype(F32)
    depth = HEADS * HD
    total = total[:, :HEADS] + (rest[:, depth : depth + 8] + rest[:, depth + 8 : depth + 16])
    attended = (
        ((numer + rest[:, :depth]).reshape(2 * ROWS, HEADS, HD) / total[:, :, None])
        .astype(BF)
        .reshape(2 * ROWS, depth)
    )

    partial = project(attended, weight).reshape(8, 2, ROWS, 256)
    parts = lax.all_to_all(partial, ("x", "yhi"), 0, 0, tiled=True)
    summed = jnp.sum(parts.astype(F32), axis=0).astype(BF)
    own = moved(lax.dynamic_index_in_dim(summed, core, 0, keepdims=False), 0)
    cross = moved(lax.dynamic_index_in_dim(summed, 1 - core, 0, keepdims=False), 1)
    even = jnp.where(first, own, cross)
    odd = jnp.where(first, cross, own)
    return jnp.concatenate([even[:, :128], odd[:, :128], even[:, 128:], odd[:, 128:]], axis=1)


def solution(mesh):
    split = Mesh(mesh.devices.reshape(SIZES), AXES)
    seq, head = ("ylo", "z"), ("x", "yhi", "core")
    return jax.shard_map(
        local,
        mesh=split,
        in_specs=(
            P(seq, head),
            P(seq, None),
            P(None, None, head),
            P(head, seq),
            P(),
            P(),
            P(),
            P(seq, None),
        ),
        out_specs=P(seq, head),
        check_vma=False,
    )
```

```python
import math

import jax
import jax.numpy as jnp
from jax import lax
from jax.experimental import pallas as pl
from jax.experimental.pallas import tpu as pltpu
from jax.sharding import Mesh, PartitionSpec as P

HD = 128
TILES = 4
EPSILON = 1e-05
NEG = -1e30
AXES = ("ylo", "zh", "zl", "x", "yhi", "core")
SIZES = (2, 8, 2, 4, 2, 2)
QUAD = ("ylo", "zl")
ROWS = 128
HEADS = 4
WIDTH = HEADS * HD
LOCAL = 200
BLOCKS = 8
SLOTS = BLOCKS * LOCAL
BF = jnp.bfloat16
F32 = jnp.float32
VMEM_LIMIT = 48 << 20


def flat(ylo, zh, zl, x, yhi, core):
    return ((((ylo * 8 + zh) * 2 + zl) * 4 + x) * 2 + yhi) * 2 + core


def everywhere(target):
    pairs = []
    for source in range(512):
        core, yhi, x = source % 2, source // 2 % 2, source // 4 % 4
        zl, zh, ylo = source // 16 % 2, source // 32 % 8, source // 256
        pairs.append((source, flat(*target(ylo, zh, zl, x, yhi, core))))
    return pairs


def swapped(value, axis):
    return lax.ppermute(value, axis, [(0, 1), (1, 0)])


def crossed(value, flip_y, flip_z):
    pairs = everywhere(
        lambda ylo, zh, zl, x, yhi, core: (ylo ^ flip_y, zh, zl ^ flip_z, x, yhi, core)
    )
    return lax.ppermute(value, AXES, pairs)


def placed(value, flip_z, flip_core):
    pairs = everywhere(
        lambda ylo, zh, zl, x, yhi, core: (
            x // 2,
            zh,
            zl ^ flip_z,
            2 * ylo + x % 2,
            yhi,
            core ^ flip_core,
        )
    )
    return lax.ppermute(value, AXES, pairs)


def vmem():
    return pl.BlockSpec(memory_space=pltpu.VMEM)


def smem():
    return pl.BlockSpec(memory_space=pltpu.SMEM)


def params():
    return pltpu.CompilerParams(vmem_limit_bytes=VMEM_LIMIT)


def prepare_kernel(q_ref, gain_ref, span_ref, o_ref):
    gain = gain_ref[...]
    for head in range(HEADS):
        columns = slice(head * HD, (head + 1) * HD)
        field = q_ref[:, columns].astype(F32)
        mean_sq = jnp.mean(field * field, axis=1, keepdims=True)
        o_ref[:, columns] = (field / jnp.sqrt(mean_sq + EPSILON) * gain).astype(BF)
    row = lax.broadcasted_iota(jnp.int32, (ROWS, HD), 0)
    lane = lax.broadcasted_iota(jnp.int32, (ROWS, HD), 1)
    begin = jnp.sum(jnp.where(row == lane, span_ref[0:1, :], 0), axis=1, keepdims=True)
    end = jnp.sum(jnp.where(row == lane, span_ref[1:2, :], 0), axis=1, keepdims=True)
    inside = (begin <= lane) & (lane < end)
    o_ref[:, WIDTH:] = jnp.where((lane <= TILES) & ~inside, NEG, 0.0).astype(BF)


def prepare(queries, q_gain, spans):
    return pl.pallas_call(
        prepare_kernel,
        in_specs=[vmem(), vmem(), vmem()],
        out_specs=vmem(),
        out_shape=jax.ShapeDtypeStruct((ROWS, WIDTH + HD), BF),
        compiler_params=params(),
        name="prepare",
    )(queries, q_gain.reshape(1, HD), spans.T)


def attend_kernel(place_ref, count_ref, q_ref, mine_ref, theirs_ref, o_ref, key_s, value_s):
    core, ylo, zl = place_ref[0], place_ref[1], place_ref[2]
    half = HD // 2
    lane = lax.broadcasted_iota(jnp.int32, (LOCAL, HD), 1)
    item = lax.broadcasted_iota(jnp.int32, (LOCAL, HD), 0)
    for block in range(BLOCKS):
        rows = slice(block * LOCAL, (block + 1) * LOCAL)
        mine, theirs = mine_ref[block], theirs_ref[block]
        left = jnp.where(core == 0, mine, theirs)
        right = jnp.where(core == 0, theirs, mine)
        key_s[rows, :HD] = jnp.concatenate([left[:, :half], right[:, :half]], axis=1)
        value_s[rows, :HD] = jnp.concatenate([left[:, half:], right[:, half:]], axis=1)
        tile = 2 * ylo + block // 4
        absent = item + ((block % 4) * 2 + zl) * LOCAL >= count_ref[tile]
        key_s[rows, HD:] = jnp.where(
            (lane == tile) | ((lane == TILES) & absent), 1.0, 0.0
        ).astype(BF)
    value_s[:, HD:] = jnp.ones((SLOTS, HD), BF)
    query_ext = q_ref[:, :, WIDTH:].reshape(4 * ROWS, HD)
    wide = lax.broadcasted_iota(jnp.int32, (4 * ROWS, HD), 1)
    totals = jnp.zeros((4 * ROWS, HD), F32)
    for head in range(HEADS):
        columns = slice(head * HD, (head + 1) * HD)
        query = q_ref[:, :, columns].reshape(4 * ROWS, HD)
        scores = lax.dot_general(
            jnp.concatenate([query, query_ext], axis=1),
            key_s[...],
            (((1,), (1,)), ((), ())),
            preferred_element_type=F32,
        )
        weights = jnp.exp2(scores * (math.log2(math.e) / math.sqrt(HD))).astype(BF)
        result = jnp.dot(weights, value_s[...], preferred_element_type=F32)
        numer = result[:, :HD].astype(BF)
        for part in range(4):
            o_ref[part ^ (2 * ylo + zl), :, columns] = numer[part * ROWS : (part + 1) * ROWS]
        totals = jnp.where(wide % HEADS == head, result[:, HD:], totals)
    high = totals.astype(BF)
    low = (totals - high.astype(F32)).astype(BF)
    packed = jnp.where(wide < HEADS, high.astype(F32), low.astype(F32)).astype(BF)
    for part in range(4):
        o_ref[part ^ (2 * ylo + zl), :, WIDTH:] = packed[part * ROWS : (part + 1) * ROWS]


def attend(place, counts, query, mine, theirs):
    return pl.pallas_call(
        attend_kernel,
        in_specs=[smem(), smem(), vmem(), vmem(), vmem()],
        out_specs=vmem(),
        out_shape=jax.ShapeDtypeStruct((4, ROWS, WIDTH + HD), BF),
        scratch_shapes=[pltpu.VMEM((SLOTS, 2 * HD), BF), pltpu.VMEM((SLOTS, 2 * HD), BF)],
        compiler_params=params(),
        name="attend",
    )(place, counts, query, mine, theirs)


def combine_kernel(x_ref, o_ref):
    summed = x_ref[0].astype(F32)
    for source in range(1, 4):
        summed = summed + x_ref[source].astype(F32)
    for head in range(HEADS):
        columns = slice(head * HD, (head + 1) * HD)
        high = summed[:, WIDTH + head : WIDTH + head + 1]
        low = summed[:, WIDTH + HEADS + head : WIDTH + HEADS + head + 1]
        o_ref[:, columns] = (summed[:, columns] / (high + low)).astype(BF)


def combine(parts):
    return pl.pallas_call(
        combine_kernel,
        in_specs=[vmem()],
        out_specs=vmem(),
        out_shape=jax.ShapeDtypeStruct((ROWS, WIDTH), BF),
        compiler_params=params(),
        name="combine",
    )(parts)


def project_kernel(own_ref, other_ref, w_hbm, o_hbm, w_s, o_s, in_sem, out_sem):
    fetch = [
        pltpu.make_async_copy(
            w_hbm.at[pl.ds(2 * step, 2)], w_s.at[pl.ds(2 * step, 2)], in_sem.at[step]
        )
        for step in range(4)
    ]
    for copy in fetch:
        copy.start()
    own = own_ref[...].reshape(4 * ROWS, WIDTH)
    other = other_ref[...].reshape(4 * ROWS, WIDTH)
    drain = []
    for step in range(4):
        fetch[step].wait()
        weight = jnp.concatenate([w_s[2 * step], w_s[2 * step + 1]], axis=1)
        result = jnp.dot(own, weight[:WIDTH], preferred_element_type=F32)
        result = result + jnp.dot(other, weight[WIDTH:], preferred_element_type=F32)
        result = result.astype(BF)
        for upper in range(2):
            for lower in range(2):
                begin = (2 * upper + lower) * ROWS
                rows = slice(begin, begin + ROWS)
                o_s[step, upper, lower, 0] = result[rows, :HD]
                o_s[step, upper, lower, 1] = result[rows, HD:]
        copy = pltpu.make_async_copy(o_s.at[step], o_hbm.at[:, step], out_sem.at[step])
        copy.start()
        drain.append(copy)
    for copy in drain:
        copy.wait()


def project(own, other, weight):
    hbm = pl.BlockSpec(memory_space=pltpu.HBM)
    return pl.pallas_call(
        project_kernel,
        in_specs=[vmem(), vmem(), hbm],
        out_specs=hbm,
        out_shape=jax.ShapeDtypeStruct((2, 4, 2, 2, ROWS, HD), BF),
        scratch_shapes=[
            pltpu.VMEM((BLOCKS, 2 * WIDTH, HD), BF),
            pltpu.VMEM((4, 2, 2, 2, ROWS, HD), BF),
            pltpu.SemaphoreType.DMA((4,)),
            pltpu.SemaphoreType.DMA((4,)),
        ],
        compiler_params=params(),
        name="project",
    )(own, other, weight)


def local(queries, vision, kv_weight, out_weight, q_gain, k_gain, tile_counts, spans):
    core = lax.axis_index("core")
    ylo = lax.axis_index("ylo")
    zl = lax.axis_index("zl")
    half = HD // 2

    kept = lax.dynamic_slice_in_dim(out_weight, core * HD, HD, axis=1)
    sent = lax.dynamic_slice_in_dim(out_weight, (1 - core) * HD, HD, axis=1)
    pair = jnp.concatenate([kept, swapped(sent, "core")], axis=0)
    weight = lax.all_gather(pair, "zh", axis=0, tiled=False)

    both = jnp.transpose(kv_weight, (0, 2, 1)).reshape(HD, vision.shape[1])
    projected = lax.dot_general(
        vision, both, (((1,), (1,)), ((), ())), preferred_element_type=F32
    )
    key_raw = projected[:, :half]
    own_squares = jnp.sum(key_raw * key_raw, axis=1)
    inverse = 1.0 / jnp.sqrt((own_squares + swapped(own_squares, "core")) / HD + EPSILON)
    gain_half = lax.dynamic_slice_in_dim(k_gain, core * half, half)
    key_half = key_raw * inverse[:, None] * gain_half[None, :]
    local_pair = jnp.concatenate([key_half, projected[:, half:]], axis=1).astype(BF)
    mine = lax.all_gather(local_pair, "zh", axis=0, tiled=False)
    theirs = swapped(mine, "core")

    query = prepare(queries, q_gain, spans)
    shared = jnp.stack(
        [query, crossed(query, 0, 1), crossed(query, 1, 0), crossed(query, 1, 1)], axis=0
    )

    place = jnp.stack([core, ylo, zl]).astype(jnp.int32)
    partial = attend(place, tile_counts, shared, mine, theirs)
    attended = combine(lax.all_to_all(partial, QUAD, 0, 0, tiled=True))
    own = lax.all_gather(attended, QUAD, axis=0, tiled=False)
    other = swapped(own, "core")

    product = project(own, other, weight).reshape(8, 2, 2, ROWS, HD)
    parts = lax.all_to_all(product, ("x", "yhi"), 0, 0, tiled=True)
    summed = jnp.sum(parts.astype(F32), axis=0).astype(BF)
    pieces = {}
    for flip_z in range(2):
        row = lax.dynamic_index_in_dim(summed, zl ^ flip_z, 0, keepdims=False)
        for flip_core in range(2):
            piece = lax.dynamic_index_in_dim(row, core ^ flip_core, 0, keepdims=False)
            pieces[flip_z, flip_core] = placed(piece, flip_z, flip_core)
    columns = []
    for side in range(2):
        for lane in range(2):
            near = jnp.where(core == lane, pieces[0, 0], pieces[0, 1])
            far = jnp.where(core == lane, pieces[1, 0], pieces[1, 1])
            columns.append(jnp.where(zl == side, near, far))
    return jnp.concatenate(columns, axis=1)


def solution(mesh):
    split = Mesh(mesh.devices.reshape(SIZES), AXES)
    seq, head = ("ylo", "zh", "zl"), ("x", "yhi", "core")
    return jax.shard_map(
        local,
        mesh=split,
        in_specs=(
            P(seq, head),
            P(seq, None),
            P(None, None, head),
            P(head, seq),
            P(),
            P(),
            P(),
            P(seq, None),
        ),
        out_specs=P(seq, head),
        check_vma=False,
    )
```

```python
import math

import jax
import jax.numpy as jnp
from jax import lax
from jax.experimental import pallas as pl
from jax.experimental.pallas import tpu as pltpu
from jax.sharding import Mesh, PartitionSpec as P

HD = 128
TILES = 4
EPSILON = 1e-05
NEG = -1e30
AXES = ("ylo", "z", "x", "yhi", "core")
SIZES = (2, 16, 4, 2, 2)
ROWS = 128
HEADS = 4
WIDTH = HEADS * HD
LOCAL = 200
BLOCKS = 16
SLOTS = BLOCKS * LOCAL
BF = jnp.bfloat16
F32 = jnp.float32


def flat(ylo, z, x, yhi, core):
    return (((ylo * 16 + z) * 4 + x) * 2 + yhi) * 2 + core


def swapped(value, axis):
    return lax.ppermute(value, axis, [(0, 1), (1, 0)])


def placed(value, flip):
    pairs = []
    for source in range(512):
        core, yhi, x, z = source % 2, source // 2 % 2, source // 4 % 4, source // 16 % 16
        target = flat(x // 2, z, 2 * (source // 256) + x % 2, yhi, core ^ flip)
        pairs.append((source, target))
    return lax.ppermute(value, AXES, pairs)


def vmem():
    return pl.BlockSpec(memory_space=pltpu.VMEM)


def smem():
    return pl.BlockSpec(memory_space=pltpu.SMEM)


def params(mib):
    return pltpu.CompilerParams(vmem_limit_bytes=mib << 20)


def prepare_kernel(q_ref, gain_ref, span_ref, o_ref):
    gain = gain_ref[...]
    for head in range(HEADS):
        columns = slice(head * HD, (head + 1) * HD)
        field = q_ref[:, columns].astype(F32)
        mean_sq = jnp.mean(field * field, axis=1, keepdims=True)
        o_ref[:, columns] = (field / jnp.sqrt(mean_sq + EPSILON) * gain).astype(BF)
    row = lax.broadcasted_iota(jnp.int32, (ROWS, HD), 0)
    lane = lax.broadcasted_iota(jnp.int32, (ROWS, HD), 1)
    begin = jnp.sum(jnp.where(row == lane, span_ref[0:1, :], 0), axis=1, keepdims=True)
    end = jnp.sum(jnp.where(row == lane, span_ref[1:2, :], 0), axis=1, keepdims=True)
    inside = (begin <= lane) & (lane < end)
    o_ref[:, WIDTH:] = jnp.where((lane <= TILES) & ~inside, NEG, 0.0).astype(BF)


def prepare(queries, q_gain, spans):
    return pl.pallas_call(
        prepare_kernel,
        in_specs=[vmem(), vmem(), vmem()],
        out_specs=vmem(),
        out_shape=jax.ShapeDtypeStruct((ROWS, WIDTH + HD), BF),
        compiler_params=params(4),
        name="prepare",
    )(queries, q_gain.reshape(1, HD), spans.T)


def attend_kernel(place_ref, count_ref, q_ref, far_ref, mine_ref, theirs_ref, o_ref, key_s, value_s):
    core, ylo = place_ref[0], place_ref[1]
    half = HD // 2
    lane = lax.broadcasted_iota(jnp.int32, (LOCAL, HD), 1)
    item = lax.broadcasted_iota(jnp.int32, (LOCAL, HD), 0)
    for block in range(BLOCKS):
        rows = slice(block * LOCAL, (block + 1) * LOCAL)
        mine, theirs = mine_ref[block], theirs_ref[block]
        left = jnp.where(core == 0, mine, theirs)
        right = jnp.where(core == 0, theirs, mine)
        key_s[rows, :HD] = jnp.concatenate([left[:, :half], right[:, :half]], axis=1)
        value_s[rows, :HD] = jnp.concatenate([left[:, half:], right[:, half:]], axis=1)
        tile = 2 * ylo + block // 8
        absent = item + (block % 8) * LOCAL >= count_ref[tile]
        key_s[rows, HD:] = jnp.where(
            (lane == tile) | ((lane == TILES) & absent), 1.0, 0.0
        ).astype(BF)
    value_s[:, HD:] = jnp.ones((SLOTS, HD), BF)
    query_ext = jnp.concatenate([q_ref[:, WIDTH:], far_ref[:, WIDTH:]], axis=0)
    wide = lax.broadcasted_iota(jnp.int32, (2 * ROWS, HD), 1)
    totals = jnp.zeros((2 * ROWS, HD), F32)
    for head in range(HEADS):
        columns = slice(head * HD, (head + 1) * HD)
        query = jnp.concatenate([q_ref[:, columns], far_ref[:, columns]], axis=0)
        scores = lax.dot_general(
            jnp.concatenate([query, query_ext], axis=1),
            key_s[...],
            (((1,), (1,)), ((), ())),
            preferred_element_type=F32,
        )
        weights = jnp.exp2(scores * (math.log2(math.e) / math.sqrt(HD))).astype(BF)
        result = jnp.dot(weights, value_s[...], preferred_element_type=F32)
        numer = result[:, :HD].astype(BF)
        o_ref[ylo, :, columns] = numer[:ROWS]
        o_ref[1 - ylo, :, columns] = numer[ROWS:]
        totals = jnp.where(wide % HEADS == head, result[:, HD:], totals)
    high = totals.astype(BF)
    low = (totals - high.astype(F32)).astype(BF)
    packed = jnp.where(wide < HEADS, high.astype(F32), low.astype(F32)).astype(BF)
    o_ref[ylo, :, WIDTH:] = packed[:ROWS]
    o_ref[1 - ylo, :, WIDTH:] = packed[ROWS:]


def attend(place, counts, query, far, mine, theirs):
    return pl.pallas_call(
        attend_kernel,
        in_specs=[smem(), smem(), vmem(), vmem(), vmem(), vmem()],
        out_specs=vmem(),
        out_shape=jax.ShapeDtypeStruct((2, ROWS, WIDTH + HD), BF),
        scratch_shapes=[pltpu.VMEM((SLOTS, 2 * HD), BF), pltpu.VMEM((SLOTS, 2 * HD), BF)],
        compiler_params=params(32),
        name="attend",
    )(place, counts, query, far, mine, theirs)


def combine_kernel(near_ref, far_ref, o_ref):
    for block in range(2):
        summed = near_ref[block].astype(F32) + far_ref[block].astype(F32)
        for head in range(HEADS):
            columns = slice(head * HD, (head + 1) * HD)
            high = summed[:, WIDTH + head : WIDTH + head + 1]
            low = summed[:, WIDTH + HEADS + head : WIDTH + HEADS + head + 1]
            rows = slice(block * ROWS, (block + 1) * ROWS)
            o_ref[rows, columns] = (summed[:, columns] / (high + low)).astype(BF)


def combine(near, far):
    return pl.pallas_call(
        combine_kernel,
        in_specs=[vmem(), vmem()],
        out_specs=vmem(),
        out_shape=jax.ShapeDtypeStruct((2 * ROWS, WIDTH), BF),
        compiler_params=params(4),
        name="combine",
    )(near, far)


def project_kernel(own_ref, other_ref, w_hbm, o_hbm, w_s, o_s, in_sem, out_sem):
    steps = BLOCKS // 2
    fetch = [
        pltpu.make_async_copy(
            w_hbm.at[pl.ds(2 * step, 2)], w_s.at[pl.ds(2 * step, 2)], in_sem.at[step]
        )
        for step in range(steps)
    ]
    for copy in fetch:
        copy.start()
    drain = []
    for step in range(steps):
        fetch[step].wait()
        weight = jnp.concatenate([w_s[2 * step], w_s[2 * step + 1]], axis=1)
        result = jnp.dot(own_ref[...], weight[:WIDTH], preferred_element_type=F32)
        result = result + jnp.dot(other_ref[...], weight[WIDTH:], preferred_element_type=F32)
        result = result.astype(BF)
        o_s[step, 0] = result[:ROWS]
        o_s[step, 1] = result[ROWS:]
        copy = pltpu.make_async_copy(
            o_s.at[step], o_hbm.at[:, step // 2, step % 2], out_sem.at[step]
        )
        copy.start()
        drain.append(copy)
    for copy in drain:
        copy.wait()


def project(own, other, weight):
    hbm = pl.BlockSpec(memory_space=pltpu.HBM)
    return pl.pallas_call(
        project_kernel,
        in_specs=[vmem(), vmem(), hbm],
        out_specs=hbm,
        out_shape=jax.ShapeDtypeStruct((2, 4, 2, ROWS, 2 * HD), BF),
        scratch_shapes=[
            pltpu.VMEM((BLOCKS, 2 * WIDTH, HD), BF),
            pltpu.VMEM((8, 2, ROWS, 2 * HD), BF),
            pltpu.SemaphoreType.DMA((8,)),
            pltpu.SemaphoreType.DMA((8,)),
        ],
        compiler_params=params(12),
        name="project",
    )(own, other, weight)


def local(queries, vision, kv_weight, out_weight, q_gain, k_gain, tile_counts, spans):
    core = lax.axis_index("core")
    ylo = lax.axis_index("ylo")
    half = HD // 2

    query = prepare(queries, q_gain, spans)
    vision, query = lax.optimization_barrier((vision, query))
    far = swapped(query, "ylo")

    kept = lax.dynamic_slice_in_dim(out_weight, core * HD, HD, axis=1)
    sent = lax.dynamic_slice_in_dim(out_weight, (1 - core) * HD, HD, axis=1)
    pair = jnp.concatenate([kept, swapped(sent, "core")], axis=0)
    weight = lax.all_gather(pair, "z", axis=0, tiled=False)

    both = jnp.transpose(kv_weight, (0, 2, 1)).reshape(HD, vision.shape[1])
    projected = lax.dot_general(
        vision, both, (((1,), (1,)), ((), ())), preferred_element_type=F32
    )
    key_raw = projected[:, :half]
    own_squares = jnp.sum(key_raw * key_raw, axis=1)
    inverse = 1.0 / jnp.sqrt((own_squares + swapped(own_squares, "core")) / HD + EPSILON)
    gain_half = lax.dynamic_slice_in_dim(k_gain, core * half, half)
    key_half = key_raw * inverse[:, None] * gain_half[None, :]
    local_pair = jnp.concatenate([key_half, projected[:, half:]], axis=1).astype(BF)
    local_pair, far = lax.optimization_barrier((local_pair, far))
    mine = lax.all_gather(local_pair, "z", axis=0, tiled=False)
    theirs = swapped(mine, "core")

    place = jnp.stack([core, ylo]).astype(jnp.int32)
    partial = attend(place, tile_counts, query, far, mine, theirs)
    own = combine(partial, swapped(partial, "ylo"))
    other = swapped(own, "core")

    product = project(own, other, weight).reshape(8, 2, ROWS, 2 * HD)
    parts = lax.all_to_all(product, ("x", "yhi"), 0, 0, tiled=True)
    summed = jnp.sum(parts.astype(F32), axis=0).astype(BF)
    same = placed(lax.dynamic_index_in_dim(summed, core, 0, keepdims=False), 0)
    cross = placed(lax.dynamic_index_in_dim(summed, 1 - core, 0, keepdims=False), 1)
    even = jnp.where(core == 0, same, cross)
    odd = jnp.where(core == 0, cross, same)
    return jnp.concatenate([even[:, :HD], odd[:, :HD], even[:, HD:], odd[:, HD:]], axis=1)


def solution(mesh):
    split = Mesh(mesh.devices.reshape(SIZES), AXES)
    seq, head = ("ylo", "z"), ("x", "yhi", "core")
    return jax.shard_map(
        local,
        mesh=split,
        in_specs=(
            P(seq, head),
            P(seq, None),
            P(None, None, head),
            P(head, seq),
            P(),
            P(),
            P(),
            P(seq, None),
        ),
        out_specs=P(seq, head),
        check_vma=False,
    )
```

```python
import math

import jax
import jax.numpy as jnp
from jax import lax
from jax.experimental import pallas as pl
from jax.experimental.pallas import tpu as pltpu
from jax.sharding import Mesh, PartitionSpec as P

HD = 128
TILES = 4
EPSILON = 1e-05
NEG = -1e30
AXES = ("ylo", "z", "x", "yhi", "core")
SIZES = (2, 16, 4, 2, 2)
ROWS = 128
HEADS = 4
WIDTH = HEADS * HD
LOCAL = 200
BLOCKS = 16
SLOTS = BLOCKS * LOCAL
BF = jnp.bfloat16
F32 = jnp.float32


def flat(ylo, z, x, yhi, core):
    return (((ylo * 16 + z) * 4 + x) * 2 + yhi) * 2 + core


def swapped(value, axis):
    return lax.ppermute(value, axis, [(0, 1), (1, 0)])


def placed(value, flip):
    pairs = []
    for source in range(512):
        core, yhi, x, z = source % 2, source // 2 % 2, source // 4 % 4, source // 16 % 16
        target = flat(x // 2, z, 2 * (source // 256) + x % 2, yhi, core ^ flip)
        pairs.append((source, target))
    return lax.ppermute(value, AXES, pairs)


def vmem():
    return pl.BlockSpec(memory_space=pltpu.VMEM)


def smem():
    return pl.BlockSpec(memory_space=pltpu.SMEM)


def params(mib):
    return pltpu.CompilerParams(vmem_limit_bytes=mib << 20)


def prepare_kernel(q_ref, gain_ref, span_ref, o_ref):
    gain = gain_ref[...]
    for head in range(HEADS):
        columns = slice(head * HD, (head + 1) * HD)
        field = q_ref[:, columns].astype(F32)
        mean_sq = jnp.mean(field * field, axis=1, keepdims=True)
        o_ref[:, columns] = (field / jnp.sqrt(mean_sq + EPSILON) * gain).astype(BF)
    row = lax.broadcasted_iota(jnp.int32, (ROWS, HD), 0)
    lane = lax.broadcasted_iota(jnp.int32, (ROWS, HD), 1)
    begin = jnp.sum(jnp.where(row == lane, span_ref[0:1, :], 0), axis=1, keepdims=True)
    end = jnp.sum(jnp.where(row == lane, span_ref[1:2, :], 0), axis=1, keepdims=True)
    inside = (begin <= lane) & (lane < end)
    o_ref[:, WIDTH:] = jnp.where((lane <= TILES) & ~inside, NEG, 0.0).astype(BF)


def prepare(queries, q_gain, spans):
    return pl.pallas_call(
        prepare_kernel,
        out_shape=jax.ShapeDtypeStruct((ROWS, WIDTH + HD), BF),
        compiler_params=params(4),
        name="prepare",
    )(queries, q_gain.reshape(1, HD), spans.T)


def column(row, count):
    width = row.shape[1]
    across = lax.broadcasted_iota(jnp.int32, (count, width), 1)
    down = lax.broadcasted_iota(jnp.int32, (count, width), 0)
    return jnp.sum(jnp.where(across == down, row, 0.0), axis=1, keepdims=True)


def pack_kernel(place_ref, x_ref, own_ref, other_ref, gain_ref, o_ref):
    mean_sq = (column(own_ref[...], LOCAL) + column(other_ref[...], LOCAL)) / HD
    gain = gain_ref[...]
    gain = jnp.where(place_ref[0] == 0, gain, jnp.concatenate([gain[:, HD // 2 :]] * 2, axis=1))
    lane = lax.broadcasted_iota(jnp.int32, (LOCAL, HD), 1)
    field = x_ref[...]
    key = field / jnp.sqrt(mean_sq + EPSILON) * gain
    o_ref[...] = jnp.where(lane < HD // 2, key, field).astype(BF)


def pack(place, projected, own_squares, other_squares, k_gain):
    return pl.pallas_call(
        pack_kernel,
        in_specs=[smem(), vmem(), vmem(), vmem(), vmem()],
        out_specs=vmem(),
        out_shape=jax.ShapeDtypeStruct((LOCAL, HD), BF),
        compiler_params=params(4),
        name="pack",
    )(
        place,
        projected,
        own_squares.reshape(1, LOCAL),
        other_squares.reshape(1, LOCAL),
        k_gain.reshape(1, HD),
    )


def attend_kernel(place_ref, count_ref, q_ref, far_ref, mine_ref, theirs_ref, o_ref, key_s, value_s):
    core, ylo = place_ref[0], place_ref[1]
    half = HD // 2
    lane = lax.broadcasted_iota(jnp.int32, (LOCAL, HD), 1)
    item = lax.broadcasted_iota(jnp.int32, (LOCAL, HD), 0)
    for block in range(BLOCKS):
        rows = slice(block * LOCAL, (block + 1) * LOCAL)
        mine, theirs = mine_ref[block], theirs_ref[block]
        left = jnp.where(core == 0, mine, theirs)
        right = jnp.where(core == 0, theirs, mine)
        key_s[rows, :HD] = jnp.concatenate([left[:, :half], right[:, :half]], axis=1)
        value_s[rows, :HD] = jnp.concatenate([left[:, half:], right[:, half:]], axis=1)
        tile = 2 * ylo + block // 8
        absent = item + (block % 8) * LOCAL >= count_ref[tile]
        key_s[rows, HD:] = jnp.where(
            (lane == tile) | ((lane == TILES) & absent), 1.0, 0.0
        ).astype(BF)
    value_s[:, HD:] = jnp.ones((SLOTS, HD), BF)
    query_ext = jnp.concatenate([q_ref[:, WIDTH:], far_ref[:, WIDTH:]], axis=0)
    wide = lax.broadcasted_iota(jnp.int32, (2 * ROWS, HD), 1)
    totals = jnp.zeros((2 * ROWS, HD), F32)
    for head in range(HEADS):
        columns = slice(head * HD, (head + 1) * HD)
        query = jnp.concatenate([q_ref[:, columns], far_ref[:, columns]], axis=0)
        scores = lax.dot_general(
            jnp.concatenate([query, query_ext], axis=1),
            key_s[...],
            (((1,), (1,)), ((), ())),
            preferred_element_type=F32,
        )
        weights = jnp.exp2(scores * (math.log2(math.e) / math.sqrt(HD))).astype(BF)
        result = jnp.dot(weights, value_s[...], preferred_element_type=F32)
        numer = result[:, :HD].astype(BF)
        o_ref[ylo, :, columns] = numer[:ROWS]
        o_ref[1 - ylo, :, columns] = numer[ROWS:]
        totals = jnp.where(wide % HEADS == head, result[:, HD:], totals)
    high = totals.astype(BF)
    low = (totals - high.astype(F32)).astype(BF)
    packed = jnp.where(wide < HEADS, high.astype(F32), low.astype(F32)).astype(BF)
    o_ref[ylo, :, WIDTH:] = packed[:ROWS]
    o_ref[1 - ylo, :, WIDTH:] = packed[ROWS:]


def attend(place, counts, query, far, mine, theirs):
    return pl.pallas_call(
        attend_kernel,
        in_specs=[smem(), smem(), vmem(), vmem(), vmem(), vmem()],
        out_specs=vmem(),
        out_shape=jax.ShapeDtypeStruct((2, ROWS, WIDTH + HD), BF),
        scratch_shapes=[pltpu.VMEM((SLOTS, 2 * HD), BF), pltpu.VMEM((SLOTS, 2 * HD), BF)],
        compiler_params=params(32),
        name="attend",
    )(place, counts, query, far, mine, theirs)


def combine_kernel(near_ref, far_ref, o_ref):
    for block in range(2):
        summed = near_ref[block].astype(F32) + far_ref[block].astype(F32)
        for head in range(HEADS):
            columns = slice(head * HD, (head + 1) * HD)
            high = summed[:, WIDTH + head : WIDTH + head + 1]
            low = summed[:, WIDTH + HEADS + head : WIDTH + HEADS + head + 1]
            rows = slice(block * ROWS, (block + 1) * ROWS)
            o_ref[rows, columns] = (summed[:, columns] / (high + low)).astype(BF)


def combine(near, far):
    return pl.pallas_call(
        combine_kernel,
        in_specs=[vmem(), vmem()],
        out_specs=vmem(),
        out_shape=jax.ShapeDtypeStruct((2 * ROWS, WIDTH), BF),
        compiler_params=params(4),
        name="combine",
    )(near, far)


def project_kernel(own_ref, other_ref, w_hbm, o_hbm, w_s, o_s, in_sem, out_sem):
    steps = BLOCKS // 2
    fetch = [
        pltpu.make_async_copy(
            w_hbm.at[pl.ds(2 * step, 2)], w_s.at[pl.ds(2 * step, 2)], in_sem.at[step]
        )
        for step in range(steps)
    ]
    for copy in fetch:
        copy.start()
    drain = []
    for step in range(steps):
        fetch[step].wait()
        weight = jnp.concatenate([w_s[2 * step], w_s[2 * step + 1]], axis=1)
        result = jnp.dot(own_ref[...], weight[:WIDTH], preferred_element_type=F32)
        result = result + jnp.dot(other_ref[...], weight[WIDTH:], preferred_element_type=F32)
        result = result.astype(BF)
        o_s[step, 0] = result[:ROWS]
        o_s[step, 1] = result[ROWS:]
        copy = pltpu.make_async_copy(
            o_s.at[step], o_hbm.at[:, step // 2, step % 2], out_sem.at[step]
        )
        copy.start()
        drain.append(copy)
    for copy in drain:
        copy.wait()


def project(own, other, weight):
    hbm = pl.BlockSpec(memory_space=pltpu.HBM)
    return pl.pallas_call(
        project_kernel,
        in_specs=[vmem(), vmem(), hbm],
        out_specs=hbm,
        out_shape=jax.ShapeDtypeStruct((2, 4, 2, ROWS, 2 * HD), BF),
        scratch_shapes=[
            pltpu.VMEM((BLOCKS, 2 * WIDTH, HD), BF),
            pltpu.VMEM((8, 2, ROWS, 2 * HD), BF),
            pltpu.SemaphoreType.DMA((8,)),
            pltpu.SemaphoreType.DMA((8,)),
        ],
        compiler_params=params(12),
        name="project",
    )(own, other, pltpu.with_memory_space_constraint(weight, pltpu.HBM))


def reduce_kernel(place_ref, x_ref, same_ref, cross_ref):
    sums = []
    for core in range(2):
        total = x_ref[0, core].astype(F32)
        for source in range(1, 8):
            total = total + x_ref[source, core].astype(F32)
        sums.append(total)
    first = place_ref[0] == 0
    same_ref[...] = jnp.where(first, sums[0], sums[1]).astype(BF)
    cross_ref[...] = jnp.where(first, sums[1], sums[0]).astype(BF)


def reduce(place, parts):
    return pl.pallas_call(
        reduce_kernel,
        in_specs=[smem(), vmem()],
        out_specs=[vmem(), vmem()],
        out_shape=[jax.ShapeDtypeStruct((ROWS, 2 * HD), BF)] * 2,
        compiler_params=params(4),
        name="reduce",
    )(place, parts)


def assemble_kernel(place_ref, same_ref, cross_ref, o_ref):
    first = place_ref[0] == 0
    same, cross = same_ref[...].astype(F32), cross_ref[...].astype(F32)
    even = jnp.where(first, same, cross).astype(BF)
    odd = jnp.where(first, cross, same).astype(BF)
    o_ref[:, 0:HD] = even[:, :HD]
    o_ref[:, HD : 2 * HD] = odd[:, :HD]
    o_ref[:, 2 * HD : 3 * HD] = even[:, HD:]
    o_ref[:, 3 * HD :] = odd[:, HD:]


def assemble(place, same, cross):
    return pl.pallas_call(
        assemble_kernel,
        in_specs=[smem(), vmem(), vmem()],
        out_shape=jax.ShapeDtypeStruct((ROWS, WIDTH), BF),
        compiler_params=params(4),
        name="assemble",
    )(place, same, cross)


def local(queries, vision, kv_weight, out_weight, q_gain, k_gain, tile_counts, spans):
    core = lax.axis_index("core")
    ylo = lax.axis_index("ylo")
    half = HD // 2

    place = jnp.stack([core, ylo]).astype(jnp.int32)

    query = prepare(queries, q_gain, spans)
    vision, query = lax.optimization_barrier((vision, query))
    far = swapped(query, "ylo")

    kept = lax.dynamic_slice_in_dim(out_weight, core * HD, HD, axis=1)
    sent = lax.dynamic_slice_in_dim(out_weight, (1 - core) * HD, HD, axis=1)
    pair = jnp.concatenate([kept, swapped(sent, "core")], axis=0)
    weight = lax.all_gather(pair, "z", axis=0, tiled=False)

    both = jnp.transpose(kv_weight, (0, 2, 1)).reshape(HD, vision.shape[1])
    projected = lax.dot_general(
        vision, both, (((1,), (1,)), ((), ())), preferred_element_type=F32
    )
    key_raw = projected[:, :half]
    own_squares = jnp.sum(key_raw * key_raw, axis=1)
    local_pair = pack(place, projected, own_squares, swapped(own_squares, "core"), k_gain)
    mine = lax.all_gather(local_pair, "z", axis=0, tiled=False)
    theirs = swapped(mine, "core")

    partial = attend(place, tile_counts, query, far, mine, theirs)
    own = combine(partial, swapped(partial, "ylo"))
    other = swapped(own, "core")

    product = project(own, other, weight).reshape(8, 2, ROWS, 2 * HD)
    parts = lax.all_to_all(product, ("x", "yhi"), 0, 0, tiled=True)
    same, cross = reduce(place, parts)
    return assemble(place, placed(same, 0), placed(cross, 1))


def solution(mesh):
    split = Mesh(mesh.devices.reshape(SIZES), AXES)
    seq, head = ("ylo", "z"), ("x", "yhi", "core")
    return jax.shard_map(
        local,
        mesh=split,
        in_specs=(
            P(seq, head),
            P(seq, None),
            P(None, None, head),
            P(head, seq),
            P(),
            P(),
            P(),
            P(seq, None),
        ),
        out_specs=P(seq, head),
        check_vma=False,
    )
```

```python
import math

import jax
import jax.numpy as jnp
from jax import lax
from jax.experimental import pallas as pl
from jax.experimental.pallas import tpu as pltpu
from jax.sharding import Mesh, PartitionSpec as P

HD = 128
TILES = 4
EPSILON = 1e-05
NEG = -1e30
AXES = ("ylo", "z", "x", "yhi", "core")
SIZES = (2, 16, 4, 2, 2)
ROWS = 128
HEADS = 4
WIDTH = HEADS * HD
LOCAL = 200
BLOCKS = 16
SLOTS = BLOCKS * LOCAL
BF = jnp.bfloat16
F32 = jnp.float32


def flat(ylo, z, x, yhi, core):
    return (((ylo * 16 + z) * 4 + x) * 2 + yhi) * 2 + core


def swapped(value, axis):
    return lax.ppermute(value, axis, [(0, 1), (1, 0)])


def placed(value, flip):
    pairs = []
    for source in range(512):
        core, yhi, x, z = source % 2, source // 2 % 2, source // 4 % 4, source // 16 % 16
        target = flat(x // 2, z, 2 * (source // 256) + x % 2, yhi, core ^ flip)
        pairs.append((source, target))
    return lax.ppermute(value, AXES, pairs)


def vmem():
    return pl.BlockSpec(memory_space=pltpu.VMEM)


def smem():
    return pl.BlockSpec(memory_space=pltpu.SMEM)


def params(mib):
    return pltpu.CompilerParams(vmem_limit_bytes=mib << 20)


def prepare_kernel(q_ref, gain_ref, span_ref, o_ref):
    gain = gain_ref[...]
    for head in range(HEADS):
        columns = slice(head * HD, (head + 1) * HD)
        field = q_ref[:, columns].astype(F32)
        mean_sq = jnp.mean(field * field, axis=1, keepdims=True)
        o_ref[:, columns] = (field / jnp.sqrt(mean_sq + EPSILON) * gain).astype(BF)
    row = lax.broadcasted_iota(jnp.int32, (ROWS, HD), 0)
    lane = lax.broadcasted_iota(jnp.int32, (ROWS, HD), 1)
    begin = jnp.sum(jnp.where(row == lane, span_ref[0:1, :], 0), axis=1, keepdims=True)
    end = jnp.sum(jnp.where(row == lane, span_ref[1:2, :], 0), axis=1, keepdims=True)
    inside = (begin <= lane) & (lane < end)
    o_ref[:, WIDTH:] = jnp.where((lane <= TILES) & ~inside, NEG, 0.0).astype(BF)


def prepare(queries, q_gain, spans):
    inputs = (queries, q_gain.reshape(1, HD), spans.T)
    return pl.pallas_call(
        prepare_kernel,
        grid=(1,),
        in_specs=[pl.BlockSpec(value.shape, lambda i: (0, 0)) for value in inputs],
        out_specs=pl.BlockSpec((ROWS, WIDTH + HD), lambda i: (0, 0)),
        out_shape=jax.ShapeDtypeStruct((ROWS, WIDTH + HD), BF),
        compiler_params=params(4),
        name="prepare",
    )(*(pltpu.with_memory_space_constraint(value, pltpu.HBM) for value in inputs))


def column(row, count):
    width = row.shape[1]
    across = lax.broadcasted_iota(jnp.int32, (count, width), 1)
    down = lax.broadcasted_iota(jnp.int32, (count, width), 0)
    return jnp.sum(jnp.where(across == down, row, 0.0), axis=1, keepdims=True)


def pack_kernel(place_ref, x_ref, own_ref, other_ref, gain_ref, o_ref):
    mean_sq = (column(own_ref[...], LOCAL) + column(other_ref[...], LOCAL)) / HD
    gain = gain_ref[...]
    gain = jnp.where(place_ref[0] == 0, gain, jnp.concatenate([gain[:, HD // 2 :]] * 2, axis=1))
    lane = lax.broadcasted_iota(jnp.int32, (LOCAL, HD), 1)
    field = x_ref[...]
    key = field / jnp.sqrt(mean_sq + EPSILON) * gain
    o_ref[...] = jnp.where(lane < HD // 2, key, field).astype(BF)


def pack(place, projected, own_squares, other_squares, k_gain):
    return pl.pallas_call(
        pack_kernel,
        in_specs=[smem(), vmem(), vmem(), vmem(), vmem()],
        out_specs=vmem(),
        out_shape=jax.ShapeDtypeStruct((LOCAL, HD), BF),
        compiler_params=params(4),
        name="pack",
    )(
        place,
        projected,
        own_squares.reshape(1, LOCAL),
        other_squares.reshape(1, LOCAL),
        k_gain.reshape(1, HD),
    )


def attend_kernel(place_ref, q_ref, far_ref, mine_ref, theirs_ref, o_ref, key_s, value_s):
    core, ylo = place_ref[0], place_ref[1]
    half = HD // 2
    lane = lax.broadcasted_iota(jnp.int32, (LOCAL, HD), 1)
    item = lax.broadcasted_iota(jnp.int32, (LOCAL, HD), 0)
    for block in range(BLOCKS):
        rows = slice(block * LOCAL, (block + 1) * LOCAL)
        mine, theirs = mine_ref[block], theirs_ref[block]
        left = jnp.where(core == 0, mine, theirs)
        right = jnp.where(core == 0, theirs, mine)
        key_s[rows, :HD] = jnp.concatenate([left[:, :half], right[:, :half]], axis=1)
        value_s[rows, :HD] = jnp.concatenate([left[:, half:], right[:, half:]], axis=1)
        tile = 2 * ylo + block // 8
        absent = item + (block % 8) * LOCAL >= place_ref[2 + tile]
        key_s[rows, HD:] = jnp.where(
            (lane == tile) | ((lane == TILES) & absent), 1.0, 0.0
        ).astype(BF)
    value_s[:, HD:] = jnp.ones((SLOTS, HD), BF)
    query_ext = jnp.concatenate([q_ref[:, WIDTH:], far_ref[:, WIDTH:]], axis=0)
    wide = lax.broadcasted_iota(jnp.int32, (2 * ROWS, HD), 1)
    totals = jnp.zeros((2 * ROWS, HD), F32)
    for head in range(HEADS):
        columns = slice(head * HD, (head + 1) * HD)
        query = jnp.concatenate([q_ref[:, columns], far_ref[:, columns]], axis=0)
        scores = lax.dot_general(
            jnp.concatenate([query, query_ext], axis=1),
            key_s[...],
            (((1,), (1,)), ((), ())),
            preferred_element_type=F32,
        )
        weights = jnp.exp2(scores * (math.log2(math.e) / math.sqrt(HD))).astype(BF)
        result = jnp.dot(weights, value_s[...], preferred_element_type=F32)
        numer = result[:, :HD].astype(BF)
        o_ref[ylo, :, columns] = numer[:ROWS]
        o_ref[1 - ylo, :, columns] = numer[ROWS:]
        totals = jnp.where(wide % HEADS == head, result[:, HD:], totals)
    high = totals.astype(BF)
    low = (totals - high.astype(F32)).astype(BF)
    packed = jnp.where(wide < HEADS, high.astype(F32), low.astype(F32)).astype(BF)
    o_ref[ylo, :, WIDTH:] = packed[:ROWS]
    o_ref[1 - ylo, :, WIDTH:] = packed[ROWS:]


def attend(place, query, far, mine, theirs):
    return pl.pallas_call(
        attend_kernel,
        in_specs=[smem(), vmem(), vmem(), vmem(), vmem()],
        out_specs=vmem(),
        out_shape=jax.ShapeDtypeStruct((2, ROWS, WIDTH + HD), BF),
        scratch_shapes=[pltpu.VMEM((SLOTS, 2 * HD), BF), pltpu.VMEM((SLOTS, 2 * HD), BF)],
        compiler_params=params(32),
        name="attend",
    )(place, query, far, mine, theirs)


def combine_kernel(near_ref, far_ref, o_ref):
    for block in range(2):
        summed = near_ref[block].astype(F32) + far_ref[block].astype(F32)
        for head in range(HEADS):
            columns = slice(head * HD, (head + 1) * HD)
            high = summed[:, WIDTH + head : WIDTH + head + 1]
            low = summed[:, WIDTH + HEADS + head : WIDTH + HEADS + head + 1]
            rows = slice(block * ROWS, (block + 1) * ROWS)
            o_ref[rows, columns] = (summed[:, columns] / (high + low)).astype(BF)


def combine(near, far):
    return pl.pallas_call(
        combine_kernel,
        in_specs=[vmem(), vmem()],
        out_specs=vmem(),
        out_shape=jax.ShapeDtypeStruct((2 * ROWS, WIDTH), BF),
        compiler_params=params(4),
        name="combine",
    )(near, far)


def project_kernel(own_ref, other_hbm, w_hbm, o_hbm, a_s, w_s, o_s, in_sem, out_sem):
    steps = BLOCKS // 2
    other = pltpu.make_async_copy(other_hbm, a_s, in_sem.at[steps])
    other.start()
    fetch = [
        pltpu.make_async_copy(
            w_hbm.at[pl.ds(2 * step, 2)], w_s.at[pl.ds(2 * step, 2)], in_sem.at[step]
        )
        for step in range(steps)
    ]
    for copy in fetch:
        copy.start()
    other.wait()
    attended = jnp.concatenate([own_ref[...], a_s[...]], axis=1)
    drain = []
    for step in range(steps):
        fetch[step].wait()
        weight = jnp.concatenate([w_s[2 * step], w_s[2 * step + 1]], axis=1)
        result = jnp.dot(attended, weight, preferred_element_type=F32).astype(BF)
        o_s[step, 0] = result[:ROWS]
        o_s[step, 1] = result[ROWS:]
        copy = pltpu.make_async_copy(
            o_s.at[step], o_hbm.at[:, step // 2, step % 2], out_sem.at[step]
        )
        copy.start()
        drain.append(copy)
    for copy in drain:
        copy.wait()


def project(own, other, weight):
    hbm = pl.BlockSpec(memory_space=pltpu.HBM)
    return pl.pallas_call(
        project_kernel,
        in_specs=[vmem(), hbm, hbm],
        out_specs=hbm,
        out_shape=jax.ShapeDtypeStruct((2, 4, 2, ROWS, 2 * HD), BF),
        scratch_shapes=[
            pltpu.VMEM((2 * ROWS, WIDTH), BF),
            pltpu.VMEM((BLOCKS, 2 * WIDTH, HD), BF),
            pltpu.VMEM((8, 2, ROWS, 2 * HD), BF),
            pltpu.SemaphoreType.DMA((9,)),
            pltpu.SemaphoreType.DMA((8,)),
        ],
        compiler_params=params(12),
        name="project",
    )(
        own,
        pltpu.with_memory_space_constraint(other, pltpu.HBM),
        pltpu.with_memory_space_constraint(weight, pltpu.HBM),
    )


def reduce_kernel(place_ref, x_ref, same_ref, cross_ref):
    sums = []
    for core in range(2):
        total = x_ref[0, core].astype(F32)
        for source in range(1, 8):
            total = total + x_ref[source, core].astype(F32)
        sums.append(total)
    first = place_ref[0] == 0
    same_ref[...] = jnp.where(first, sums[0], sums[1]).astype(BF)
    cross_ref[...] = jnp.where(first, sums[1], sums[0]).astype(BF)


def reduce(place, parts):
    return pl.pallas_call(
        reduce_kernel,
        in_specs=[smem(), vmem()],
        out_specs=[vmem(), vmem()],
        out_shape=[jax.ShapeDtypeStruct((ROWS, 2 * HD), BF)] * 2,
        compiler_params=params(4),
        name="reduce",
    )(place, parts)


def assemble_kernel(place_ref, same_ref, cross_ref, o_ref):
    first = place_ref[0] == 0
    same, cross = same_ref[...].astype(F32), cross_ref[...].astype(F32)
    even = jnp.where(first, same, cross).astype(BF)
    odd = jnp.where(first, cross, same).astype(BF)
    o_ref[:, 0:HD] = even[:, :HD]
    o_ref[:, HD : 2 * HD] = odd[:, :HD]
    o_ref[:, 2 * HD : 3 * HD] = even[:, HD:]
    o_ref[:, 3 * HD :] = odd[:, HD:]


def assemble(place, same, cross):
    return pl.pallas_call(
        assemble_kernel,
        in_specs=[smem(), vmem(), vmem()],
        out_shape=jax.ShapeDtypeStruct((ROWS, WIDTH), BF),
        compiler_params=params(4),
        name="assemble",
    )(place, same, cross)


def local(queries, vision, kv_weight, out_weight, q_gain, k_gain, tile_counts, spans):
    core = lax.axis_index("core")
    ylo = lax.axis_index("ylo")
    half = HD // 2

    place = jnp.concatenate([jnp.stack([core, ylo]).astype(jnp.int32), tile_counts])

    query = prepare(queries, q_gain, spans)

    kept = lax.dynamic_slice_in_dim(out_weight, core * HD, HD, axis=1)
    sent = lax.dynamic_slice_in_dim(out_weight, (1 - core) * HD, HD, axis=1)
    got, query = lax.optimization_barrier((swapped(sent, "core"), query))
    pair = jnp.concatenate([kept, got], axis=0)
    far = swapped(query, "ylo")
    weight = lax.all_gather(pair, "z", axis=0, tiled=False)

    both = jnp.transpose(kv_weight, (0, 2, 1)).reshape(HD, vision.shape[1])
    projected = lax.dot_general(
        vision, both, (((1,), (1,)), ((), ())), preferred_element_type=F32
    )
    projected, far = lax.optimization_barrier((projected, far))
    key_raw = projected[:, :half]
    own_squares = jnp.sum(key_raw * key_raw, axis=1)
    local_pair = pack(place, projected, own_squares, swapped(own_squares, "core"), k_gain)
    mine = lax.all_gather(local_pair, "z", axis=0, tiled=False)
    theirs = swapped(mine, "core")

    partial = attend(place, query, far, mine, theirs)
    own = combine(partial, swapped(partial, "ylo"))
    other = swapped(own, "core")

    product = project(own, other, weight).reshape(8, 2, ROWS, 2 * HD)
    parts = lax.all_to_all(product, ("x", "yhi"), 0, 0, tiled=True)
    same, cross = reduce(place, parts)
    return assemble(place, placed(same, 0), placed(cross, 1))


def solution(mesh):
    split = Mesh(mesh.devices.reshape(SIZES), AXES)
    seq, head = ("ylo", "z"), ("x", "yhi", "core")
    return jax.shard_map(
        local,
        mesh=split,
        in_specs=(
            P(seq, head),
            P(seq, None),
            P(None, None, head),
            P(head, seq),
            P(),
            P(),
            P(),
            P(seq, None),
        ),
        out_specs=P(seq, head),
        check_vma=False,
    )
```

```python
import math

import jax
import jax.numpy as jnp
from jax import lax
from jax.experimental import pallas as pl
from jax.experimental.pallas import tpu as pltpu
from jax.sharding import Mesh, PartitionSpec as P

HD = 128
TILES = 4
EPSILON = 1e-05
NEG = -1e30
AXES = ("ylo", "z", "x", "yhi", "core")
SIZES = (2, 16, 4, 2, 2)
ROWS = 128
HEADS = 4
WIDTH = HEADS * HD
LOCAL = 200
BLOCKS = 16
SLOTS = BLOCKS * LOCAL
BF = jnp.bfloat16
F32 = jnp.float32


def flat(ylo, z, x, yhi, core):
    return (((ylo * 16 + z) * 4 + x) * 2 + yhi) * 2 + core


def swapped(value, axis):
    return lax.ppermute(value, axis, [(0, 1), (1, 0)])


def placed(value):
    pairs = []
    for source in range(512):
        core, yhi, x, z = source % 2, source // 2 % 2, source // 4 % 4, source // 16 % 16
        target = flat(x // 2, z, 2 * (source // 256) + x % 2, yhi, core)
        pairs.append((source, target))
    return lax.ppermute(value, AXES, pairs)


def vmem():
    return pl.BlockSpec(memory_space=pltpu.VMEM)


def smem():
    return pl.BlockSpec(memory_space=pltpu.SMEM)


def params(mib):
    return pltpu.CompilerParams(vmem_limit_bytes=mib << 20)


def prepare_kernel(q_ref, gain_ref, span_ref, o_ref):
    gain = gain_ref[...]
    for head in range(HEADS):
        columns = slice(head * HD, (head + 1) * HD)
        field = q_ref[:, columns].astype(F32)
        mean_sq = jnp.mean(field * field, axis=1, keepdims=True)
        o_ref[:, columns] = (field / jnp.sqrt(mean_sq + EPSILON) * gain).astype(BF)
    row = lax.broadcasted_iota(jnp.int32, (ROWS, HD), 0)
    lane = lax.broadcasted_iota(jnp.int32, (ROWS, HD), 1)
    begin = jnp.sum(jnp.where(row == lane, span_ref[0:1, :], 0), axis=1, keepdims=True)
    end = jnp.sum(jnp.where(row == lane, span_ref[1:2, :], 0), axis=1, keepdims=True)
    inside = (begin <= lane) & (lane < end)
    o_ref[:, WIDTH:] = jnp.where((lane <= TILES) & ~inside, NEG, 0.0).astype(BF)


def prepare(queries, q_gain, spans):
    inputs = (queries, q_gain.reshape(1, HD), spans.T)
    return pl.pallas_call(
        prepare_kernel,
        grid=(1,),
        in_specs=[pl.BlockSpec(value.shape, lambda i: (0, 0)) for value in inputs],
        out_specs=pl.BlockSpec((ROWS, WIDTH + HD), lambda i: (0, 0)),
        out_shape=jax.ShapeDtypeStruct((ROWS, WIDTH + HD), BF),
        compiler_params=params(4),
        name="prepare",
    )(*(pltpu.with_memory_space_constraint(value, pltpu.HBM) for value in inputs))


def column(row, count):
    width = row.shape[1]
    across = lax.broadcasted_iota(jnp.int32, (count, width), 1)
    down = lax.broadcasted_iota(jnp.int32, (count, width), 0)
    return jnp.sum(jnp.where(across == down, row, 0.0), axis=1, keepdims=True)


def pack_kernel(place_ref, x_ref, own_ref, other_ref, gain_ref, o_ref):
    mean_sq = (column(own_ref[...], LOCAL) + column(other_ref[...], LOCAL)) / HD
    gain = gain_ref[...]
    gain = jnp.where(place_ref[0] == 0, gain, jnp.concatenate([gain[:, HD // 2 :]] * 2, axis=1))
    lane = lax.broadcasted_iota(jnp.int32, (LOCAL, HD), 1)
    field = x_ref[...]
    key = field / jnp.sqrt(mean_sq + EPSILON) * gain
    o_ref[...] = jnp.where(lane < HD // 2, key, field).astype(BF)


def pack(place, projected, own_squares, other_squares, k_gain):
    return pl.pallas_call(
        pack_kernel,
        in_specs=[smem(), vmem(), vmem(), vmem(), vmem()],
        out_specs=vmem(),
        out_shape=jax.ShapeDtypeStruct((LOCAL, HD), BF),
        compiler_params=params(4),
        name="pack",
    )(
        place,
        projected,
        own_squares.reshape(1, LOCAL),
        other_squares.reshape(1, LOCAL),
        k_gain.reshape(1, HD),
    )


def attend_kernel(place_ref, q_ref, far_ref, mine_ref, theirs_ref, o_ref, key_s, value_s):
    core, ylo = place_ref[0], place_ref[1]
    half = HD // 2
    lane = lax.broadcasted_iota(jnp.int32, (LOCAL, HD), 1)
    item = lax.broadcasted_iota(jnp.int32, (LOCAL, HD), 0)
    for block in range(BLOCKS):
        rows = slice(block * LOCAL, (block + 1) * LOCAL)
        mine, theirs = mine_ref[block], theirs_ref[block]
        left = jnp.where(core == 0, mine, theirs)
        right = jnp.where(core == 0, theirs, mine)
        key_s[rows, :HD] = jnp.concatenate([left[:, :half], right[:, :half]], axis=1)
        value_s[rows, :HD] = jnp.concatenate([left[:, half:], right[:, half:]], axis=1)
        tile = 2 * ylo + block // 8
        absent = item + (block % 8) * LOCAL >= place_ref[2 + tile]
        key_s[rows, HD:] = jnp.where(
            (lane == tile) | ((lane == TILES) & absent), 1.0, 0.0
        ).astype(BF)
    value_s[:, HD:] = jnp.ones((SLOTS, HD), BF)
    query_ext = jnp.concatenate([q_ref[:, WIDTH:], far_ref[:, WIDTH:]], axis=0)
    wide = lax.broadcasted_iota(jnp.int32, (2 * ROWS, HD), 1)
    totals = jnp.zeros((2 * ROWS, HD), F32)
    for head in range(HEADS):
        columns = slice(head * HD, (head + 1) * HD)
        query = jnp.concatenate([q_ref[:, columns], far_ref[:, columns]], axis=0)
        scores = lax.dot_general(
            jnp.concatenate([query, query_ext], axis=1),
            key_s[...],
            (((1,), (1,)), ((), ())),
            preferred_element_type=F32,
        )
        weights = jnp.exp2(scores * (math.log2(math.e) / math.sqrt(HD))).astype(BF)
        result = jnp.dot(weights, value_s[...], preferred_element_type=F32)
        numer = result[:, :HD].astype(BF)
        o_ref[ylo, :, columns] = numer[:ROWS]
        o_ref[1 - ylo, :, columns] = numer[ROWS:]
        totals = jnp.where(wide % HEADS == head, result[:, HD:], totals)
    high = totals.astype(BF)
    low = (totals - high.astype(F32)).astype(BF)
    packed = jnp.where(wide < HEADS, high.astype(F32), low.astype(F32)).astype(BF)
    o_ref[ylo, :, WIDTH:] = packed[:ROWS]
    o_ref[1 - ylo, :, WIDTH:] = packed[ROWS:]


def attend(place, query, far, mine, theirs):
    return pl.pallas_call(
        attend_kernel,
        in_specs=[smem(), vmem(), vmem(), vmem(), vmem()],
        out_specs=vmem(),
        out_shape=jax.ShapeDtypeStruct((2, ROWS, WIDTH + HD), BF),
        scratch_shapes=[pltpu.VMEM((SLOTS, 2 * HD), BF), pltpu.VMEM((SLOTS, 2 * HD), BF)],
        compiler_params=params(32),
        name="attend",
    )(place, query, far, mine, theirs)


def combine_kernel(near_ref, far_ref, o_ref):
    for block in range(2):
        summed = near_ref[block].astype(F32) + far_ref[block].astype(F32)
        for head in range(HEADS):
            columns = slice(head * HD, (head + 1) * HD)
            high = summed[:, WIDTH + head : WIDTH + head + 1]
            low = summed[:, WIDTH + HEADS + head : WIDTH + HEADS + head + 1]
            rows = slice(block * ROWS, (block + 1) * ROWS)
            o_ref[rows, columns] = (summed[:, columns] / (high + low)).astype(BF)


def combine(near, far):
    return pl.pallas_call(
        combine_kernel,
        in_specs=[vmem(), vmem()],
        out_specs=vmem(),
        out_shape=jax.ShapeDtypeStruct((2 * ROWS, WIDTH), BF),
        compiler_params=params(4),
        name="combine",
    )(near, far)


def project_kernel(own_ref, other_hbm, w_hbm, o_hbm, a_s, w_s, o_s, in_sem, out_sem):
    steps = BLOCKS // 2
    other = pltpu.make_async_copy(other_hbm, a_s, in_sem.at[steps])
    other.start()
    fetch = [
        pltpu.make_async_copy(
            w_hbm.at[pl.ds(2 * step, 2)], w_s.at[pl.ds(2 * step, 2)], in_sem.at[step]
        )
        for step in range(steps)
    ]
    for copy in fetch:
        copy.start()
    other.wait()
    attended = jnp.concatenate([own_ref[...], a_s[...]], axis=1)
    drain = []
    for step in range(steps):
        fetch[step].wait()
        weight = jnp.concatenate([w_s[2 * step], w_s[2 * step + 1]], axis=1)
        result = jnp.dot(attended, weight, preferred_element_type=F32).astype(BF)
        o_s[step, 0] = result[:ROWS]
        o_s[step, 1] = result[ROWS:]
        copy = pltpu.make_async_copy(
            o_s.at[step], o_hbm.at[:, step // 2, step % 2], out_sem.at[step]
        )
        copy.start()
        drain.append(copy)
    for copy in drain:
        copy.wait()


def project(own, other, weight):
    hbm = pl.BlockSpec(memory_space=pltpu.HBM)
    return pl.pallas_call(
        project_kernel,
        in_specs=[vmem(), hbm, hbm],
        out_specs=hbm,
        out_shape=jax.ShapeDtypeStruct((2, 4, 2, ROWS, 2 * HD), BF),
        scratch_shapes=[
            pltpu.VMEM((2 * ROWS, WIDTH), BF),
            pltpu.VMEM((BLOCKS, 2 * WIDTH, HD), BF),
            pltpu.VMEM((8, 2, ROWS, 2 * HD), BF),
            pltpu.SemaphoreType.DMA((9,)),
            pltpu.SemaphoreType.DMA((8,)),
        ],
        compiler_params=params(12),
        name="project",
    )(
        own,
        pltpu.with_memory_space_constraint(other, pltpu.HBM),
        pltpu.with_memory_space_constraint(weight, pltpu.HBM),
    )


def reduce_kernel(x_ref, o_ref):
    for core in range(2):
        total = x_ref[core].astype(F32)
        for source in range(1, 8):
            total = total + x_ref[2 * source + core].astype(F32)
        total = total.astype(BF)
        o_ref[:, core * HD : (core + 1) * HD] = total[:, :HD]
        o_ref[:, (2 + core) * HD : (3 + core) * HD] = total[:, HD:]


def reduce(parts):
    return pl.pallas_call(
        reduce_kernel,
        in_specs=[vmem()],
        out_specs=vmem(),
        out_shape=jax.ShapeDtypeStruct((ROWS, WIDTH), BF),
        compiler_params=params(4),
        name="reduce",
    )(parts)


def local(queries, vision, kv_weight, out_weight, q_gain, k_gain, tile_counts, spans):
    core = lax.axis_index("core")
    ylo = lax.axis_index("ylo")
    half = HD // 2

    place = jnp.concatenate([jnp.stack([core, ylo]).astype(jnp.int32), tile_counts])

    query = prepare(queries, q_gain, spans)

    kept = lax.dynamic_slice_in_dim(out_weight, core * HD, HD, axis=1)
    sent = lax.dynamic_slice_in_dim(out_weight, (1 - core) * HD, HD, axis=1)
    got, query = lax.optimization_barrier((swapped(sent, "core"), query))
    pair = jnp.concatenate([kept, got], axis=0)
    far = swapped(query, "ylo")
    weight = lax.all_gather(pair, "z", axis=0, tiled=False)

    both = jnp.transpose(kv_weight, (0, 2, 1)).reshape(HD, vision.shape[1])
    projected = lax.dot_general(
        vision, both, (((1,), (1,)), ((), ())), preferred_element_type=F32
    )
    projected, far = lax.optimization_barrier((projected, far))
    key_raw = projected[:, :half]
    own_squares = jnp.sum(key_raw * key_raw, axis=1)
    local_pair = pack(place, projected, own_squares, swapped(own_squares, "core"), k_gain)
    mine = lax.all_gather(local_pair, "z", axis=0, tiled=False)
    theirs = swapped(mine, "core")

    partial = attend(place, query, far, mine, theirs)
    own = combine(partial, swapped(partial, "ylo"))
    other = swapped(own, "core")

    product = project(own, other, weight).reshape(16, ROWS, 2 * HD)
    parts = lax.all_to_all(product, ("x", "yhi", "core"), 0, 0, tiled=True)
    return placed(reduce(parts))


def solution(mesh):
    split = Mesh(mesh.devices.reshape(SIZES), AXES)
    seq, head = ("ylo", "z"), ("x", "yhi", "core")
    return jax.shard_map(
        local,
        mesh=split,
        in_specs=(
            P(seq, head),
            P(seq, None),
            P(None, None, head),
            P(head, seq),
            P(),
            P(),
            P(),
            P(seq, None),
        ),
        out_specs=P(seq, head),
        check_vma=False,
    )
```

```python
import math

import jax
import jax.numpy as jnp
from jax import lax
from jax.experimental import pallas as pl
from jax.experimental.pallas import tpu as pltpu
from jax.sharding import Mesh, PartitionSpec as P

HD = 128
TILES = 4
EPSILON = 1e-05
NEG = -1e30
AXES = ("ylo", "z", "xh", "xl", "yhi", "core")
SIZES = (2, 16, 2, 2, 2, 2)
ROWS = 128
HEADS = 4
WIDTH = HEADS * HD
LOCAL = 200
BLOCKS = 16
SLOTS = BLOCKS * LOCAL
BF = jnp.bfloat16
F32 = jnp.float32


def flat(ylo, z, x, yhi, core):
    return (((ylo * 16 + z) * 4 + x) * 2 + yhi) * 2 + core


def swapped(value, axis):
    return lax.ppermute(value, axis, [(0, 1), (1, 0)])


def placed(value):
    pairs = []
    for source in range(512):
        core, yhi, x, z = source % 2, source // 2 % 2, source // 4 % 4, source // 16 % 16
        target = flat(x // 2, z, 2 * (source // 256) + x % 2, yhi, core)
        pairs.append((source, target))
    return lax.ppermute(value, AXES, pairs)


def vmem():
    return pl.BlockSpec(memory_space=pltpu.VMEM)


def smem():
    return pl.BlockSpec(memory_space=pltpu.SMEM)


def params(mib):
    return pltpu.CompilerParams(vmem_limit_bytes=mib << 20)


def prepare_kernel(q_ref, gain_ref, span_ref, o_ref):
    gain = gain_ref[...]
    for head in range(HEADS):
        columns = slice(head * HD, (head + 1) * HD)
        field = q_ref[:, columns].astype(F32)
        mean_sq = jnp.mean(field * field, axis=1, keepdims=True)
        o_ref[:, columns] = (field / jnp.sqrt(mean_sq + EPSILON) * gain).astype(BF)
    row = lax.broadcasted_iota(jnp.int32, (ROWS, HD), 0)
    lane = lax.broadcasted_iota(jnp.int32, (ROWS, HD), 1)
    begin = jnp.sum(jnp.where(row == lane, span_ref[0:1, :], 0), axis=1, keepdims=True)
    end = jnp.sum(jnp.where(row == lane, span_ref[1:2, :], 0), axis=1, keepdims=True)
    inside = (begin <= lane) & (lane < end)
    o_ref[:, WIDTH:] = jnp.where((lane <= TILES) & ~inside, NEG, 0.0).astype(BF)


def prepare(queries, q_gain, spans):
    inputs = (queries, q_gain.reshape(1, HD), spans.T)
    return pl.pallas_call(
        prepare_kernel,
        grid=(1,),
        in_specs=[pl.BlockSpec(value.shape, lambda i: (0, 0)) for value in inputs],
        out_specs=pl.BlockSpec((ROWS, WIDTH + HD), lambda i: (0, 0)),
        out_shape=jax.ShapeDtypeStruct((ROWS, WIDTH + HD), BF),
        compiler_params=params(4),
        name="prepare",
    )(*(pltpu.with_memory_space_constraint(value, pltpu.HBM) for value in inputs))


def column(row, count):
    width = row.shape[1]
    across = lax.broadcasted_iota(jnp.int32, (count, width), 1)
    down = lax.broadcasted_iota(jnp.int32, (count, width), 0)
    return jnp.sum(jnp.where(across == down, row, 0.0), axis=1, keepdims=True)


def pack_kernel(place_ref, x_ref, own_ref, other_ref, gain_ref, o_ref):
    mean_sq = (column(own_ref[...], LOCAL) + column(other_ref[...], LOCAL)) / HD
    gain = gain_ref[...]
    gain = jnp.where(place_ref[0] == 0, gain, jnp.concatenate([gain[:, HD // 2 :]] * 2, axis=1))
    lane = lax.broadcasted_iota(jnp.int32, (LOCAL, HD), 1)
    field = x_ref[...]
    key = field / jnp.sqrt(mean_sq + EPSILON) * gain
    o_ref[...] = jnp.where(lane < HD // 2, key, field).astype(BF)


def pack(place, projected, own_squares, other_squares, k_gain):
    return pl.pallas_call(
        pack_kernel,
        in_specs=[smem(), vmem(), vmem(), vmem(), vmem()],
        out_specs=vmem(),
        out_shape=jax.ShapeDtypeStruct((LOCAL, HD), BF),
        compiler_params=params(4),
        name="pack",
    )(
        place,
        projected,
        own_squares.reshape(1, LOCAL),
        other_squares.reshape(1, LOCAL),
        k_gain.reshape(1, HD),
    )


def attend_kernel(place_ref, q_ref, far_ref, mine_ref, theirs_ref, o_ref, key_s, value_s):
    core, ylo = place_ref[0], place_ref[1]
    half = HD // 2
    lane = lax.broadcasted_iota(jnp.int32, (LOCAL, HD), 1)
    item = lax.broadcasted_iota(jnp.int32, (LOCAL, HD), 0)
    for block in range(BLOCKS):
        rows = slice(block * LOCAL, (block + 1) * LOCAL)
        mine, theirs = mine_ref[block], theirs_ref[block]
        left = jnp.where(core == 0, mine, theirs)
        right = jnp.where(core == 0, theirs, mine)
        key_s[rows, :HD] = jnp.concatenate([left[:, :half], right[:, :half]], axis=1)
        value_s[rows, :HD] = jnp.concatenate([left[:, half:], right[:, half:]], axis=1)
        tile = 2 * ylo + block // 8
        absent = item + (block % 8) * LOCAL >= place_ref[2 + tile]
        key_s[rows, HD:] = jnp.where(
            (lane == tile) | ((lane == TILES) & absent), 1.0, 0.0
        ).astype(BF)
    value_s[:, HD:] = jnp.ones((SLOTS, HD), BF)
    query_ext = jnp.concatenate([q_ref[:, WIDTH:], far_ref[:, WIDTH:]], axis=0)
    wide = lax.broadcasted_iota(jnp.int32, (2 * ROWS, HD), 1)
    totals = jnp.zeros((2 * ROWS, HD), F32)
    for head in range(HEADS):
        columns = slice(head * HD, (head + 1) * HD)
        query = jnp.concatenate([q_ref[:, columns], far_ref[:, columns]], axis=0)
        scores = lax.dot_general(
            jnp.concatenate([query, query_ext], axis=1),
            key_s[...],
            (((1,), (1,)), ((), ())),
            preferred_element_type=F32,
        )
        weights = jnp.exp2(scores * (math.log2(math.e) / math.sqrt(HD))).astype(BF)
        result = jnp.dot(weights, value_s[...], preferred_element_type=F32)
        numer = result[:, :HD].astype(BF)
        o_ref[ylo, :, columns] = numer[:ROWS]
        o_ref[1 - ylo, :, columns] = numer[ROWS:]
        totals = jnp.where(wide % HEADS == head, result[:, HD:], totals)
    high = totals.astype(BF)
    low = (totals - high.astype(F32)).astype(BF)
    packed = jnp.where(wide < HEADS, high.astype(F32), low.astype(F32)).astype(BF)
    o_ref[ylo, :, WIDTH:] = packed[:ROWS]
    o_ref[1 - ylo, :, WIDTH:] = packed[ROWS:]


def attend(place, query, far, mine, theirs):
    return pl.pallas_call(
        attend_kernel,
        in_specs=[smem(), vmem(), vmem(), vmem(), vmem()],
        out_specs=vmem(),
        out_shape=jax.ShapeDtypeStruct((2, ROWS, WIDTH + HD), BF),
        scratch_shapes=[pltpu.VMEM((SLOTS, 2 * HD), BF), pltpu.VMEM((SLOTS, 2 * HD), BF)],
        compiler_params=params(32),
        name="attend",
    )(place, query, far, mine, theirs)


def combine_kernel(near_ref, far_ref, o_ref):
    for block in range(2):
        summed = near_ref[block].astype(F32) + far_ref[block].astype(F32)
        for head in range(HEADS):
            columns = slice(head * HD, (head + 1) * HD)
            high = summed[:, WIDTH + head : WIDTH + head + 1]
            low = summed[:, WIDTH + HEADS + head : WIDTH + HEADS + head + 1]
            rows = slice(block * ROWS, (block + 1) * ROWS)
            o_ref[rows, columns] = (summed[:, columns] / (high + low)).astype(BF)


def combine(near, far):
    return pl.pallas_call(
        combine_kernel,
        in_specs=[vmem(), vmem()],
        out_specs=vmem(),
        out_shape=jax.ShapeDtypeStruct((2 * ROWS, WIDTH), BF),
        compiler_params=params(4),
        name="combine",
    )(near, far)


def reduce_kernel(x_ref, o_ref):
    for core in range(2):
        for side in range(2):
            total = jnp.zeros((HD, ROWS), F32)
            for source in range(16):
                if source // 2 % 2 == core:
                    total = total + x_ref[source, side].astype(F32)
            begin = (2 * side + core) * HD
            o_ref[:, begin : begin + HD] = total.T.astype(BF)


def reduce(parts):
    return pl.pallas_call(
        reduce_kernel,
        in_specs=[vmem()],
        out_specs=vmem(),
        out_shape=jax.ShapeDtypeStruct((ROWS, WIDTH), BF),
        compiler_params=params(4),
        name="reduce",
    )(parts)


def local(queries, vision, kv_weight, out_weight, q_gain, k_gain, tile_counts, spans):
    core = lax.axis_index("core")
    ylo = lax.axis_index("ylo")
    half = HD // 2

    place = jnp.concatenate([jnp.stack([core, ylo]).astype(jnp.int32), tile_counts])

    query = prepare(queries, q_gain, spans)

    kept = lax.dynamic_slice_in_dim(out_weight, core * HD, HD, axis=1)
    sent = lax.dynamic_slice_in_dim(out_weight, (1 - core) * HD, HD, axis=1)
    got, query = lax.optimization_barrier((swapped(sent, "core"), query))
    pair = jnp.concatenate([kept, got], axis=0)
    far = swapped(query, "ylo")
    weight = lax.all_gather(pair, "z", axis=0, tiled=False)

    both = jnp.transpose(kv_weight, (0, 2, 1)).reshape(HD, vision.shape[1])
    projected = lax.dot_general(
        vision, both, (((1,), (1,)), ((), ())), preferred_element_type=F32
    )
    projected, far = lax.optimization_barrier((projected, far))
    key_raw = projected[:, :half]
    own_squares = jnp.sum(key_raw * key_raw, axis=1)
    local_pair = pack(place, projected, own_squares, swapped(own_squares, "core"), k_gain)
    mine = lax.all_gather(local_pair, "z", axis=0, tiled=False)
    theirs = swapped(mine, "core")

    partial = attend(place, query, far, mine, theirs)
    own = combine(partial, swapped(partial, "ylo"))
    other = swapped(own, "core")

    attended = jnp.concatenate([own, other], axis=1).reshape(2, ROWS, 2 * WIDTH)
    split = weight.reshape(8, 2, 2 * WIDTH, HD)
    product = jnp.einsum("rmk,jtkn->jrtnm", attended, split, preferred_element_type=F32)
    product = product.astype(BF).reshape(16, 2, HD, ROWS)
    parts = lax.all_to_all(product, ("xl", "yhi", "core", "xh"), 0, 0, tiled=True)
    return placed(reduce(parts))


def solution(mesh):
    split = Mesh(mesh.devices.reshape(SIZES), AXES)
    seq, head = ("ylo", "z"), ("xh", "xl", "yhi", "core")
    return jax.shard_map(
        local,
        mesh=split,
        in_specs=(
            P(seq, head),
            P(seq, None),
            P(None, None, head),
            P(head, seq),
            P(),
            P(),
            P(),
            P(seq, None),
        ),
        out_specs=P(seq, head),
        check_vma=False,
    )
```

```python
import math

import jax
import jax.numpy as jnp
from jax import lax
from jax.experimental import pallas as pl
from jax.experimental.pallas import tpu as pltpu
from jax.sharding import Mesh, PartitionSpec as P

HD = 128
TILES = 4
EPSILON = 1e-05
NEG = -1e30
AXES = ("ylo", "z", "xh", "xl", "yhi", "core")
SIZES = (2, 16, 2, 2, 2, 2)
ROWS = 128
HEADS = 4
WIDTH = HEADS * HD
LOCAL = 200
BLOCKS = 16
SLOTS = BLOCKS * LOCAL
BF = jnp.bfloat16
F32 = jnp.float32


def flat(ylo, z, x, yhi, core):
    return (((ylo * 16 + z) * 4 + x) * 2 + yhi) * 2 + core


def swapped(value, axis):
    return lax.ppermute(value, axis, [(0, 1), (1, 0)])


def placed(value):
    pairs = []
    for source in range(512):
        core, yhi, x, z = source % 2, source // 2 % 2, source // 4 % 4, source // 16 % 16
        target = flat(x // 2, z, 2 * (source // 256) + x % 2, yhi, core)
        pairs.append((source, target))
    return lax.ppermute(value, AXES, pairs)


def vmem():
    return pl.BlockSpec(memory_space=pltpu.VMEM)


def smem():
    return pl.BlockSpec(memory_space=pltpu.SMEM)


def params(mib):
    return pltpu.CompilerParams(vmem_limit_bytes=mib << 20)


def prepare_kernel(q_ref, gain_ref, span_ref, o_ref):
    gain = gain_ref[...]
    for head in range(HEADS):
        columns = slice(head * HD, (head + 1) * HD)
        field = q_ref[:, columns].astype(F32)
        mean_sq = jnp.mean(field * field, axis=1, keepdims=True)
        o_ref[:, columns] = (field / jnp.sqrt(mean_sq + EPSILON) * gain).astype(BF)
    row = lax.broadcasted_iota(jnp.int32, (ROWS, HD), 0)
    lane = lax.broadcasted_iota(jnp.int32, (ROWS, HD), 1)
    begin = jnp.sum(jnp.where(row == lane, span_ref[0:1, :], 0), axis=1, keepdims=True)
    end = jnp.sum(jnp.where(row == lane, span_ref[1:2, :], 0), axis=1, keepdims=True)
    inside = (begin <= lane) & (lane < end)
    o_ref[:, WIDTH:] = jnp.where((lane <= TILES) & ~inside, NEG, 0.0).astype(BF)


def prepare(queries, q_gain, spans):
    inputs = (queries, q_gain.reshape(1, HD), spans.T)
    return pl.pallas_call(
        prepare_kernel,
        grid=(1,),
        in_specs=[pl.BlockSpec(value.shape, lambda i: (0, 0)) for value in inputs],
        out_specs=pl.BlockSpec((ROWS, WIDTH + HD), lambda i: (0, 0)),
        out_shape=jax.ShapeDtypeStruct((ROWS, WIDTH + HD), BF),
        compiler_params=params(4),
        name="prepare",
    )(*(pltpu.with_memory_space_constraint(value, pltpu.HBM) for value in inputs))


def attend_kernel(place_ref, q_ref, far_ref, gain_ref, mine_ref, theirs_ref, o_ref, key_s, value_s):
    core, ylo = place_ref[0], place_ref[1]
    half = HD // 2
    gain = gain_ref[...]
    lane = lax.broadcasted_iota(jnp.int32, (LOCAL, HD), 1)
    item = lax.broadcasted_iota(jnp.int32, (LOCAL, HD), 0)
    for block in range(BLOCKS):
        rows = slice(block * LOCAL, (block + 1) * LOCAL)
        mine, theirs = mine_ref[block], theirs_ref[block]
        left = jnp.where(core == 0, mine, theirs)
        right = jnp.where(core == 0, theirs, mine)
        key = jnp.concatenate([left[:, :half], right[:, :half]], axis=1).astype(F32)
        mean_sq = jnp.mean(key * key, axis=1, keepdims=True)
        key_s[rows, :HD] = (key * lax.rsqrt(mean_sq + EPSILON) * gain).astype(BF)
        value_s[rows, :HD] = jnp.concatenate([left[:, half:], right[:, half:]], axis=1)
        tile = 2 * ylo + block // 8
        absent = item + (block % 8) * LOCAL >= place_ref[2 + tile]
        key_s[rows, HD:] = jnp.where(
            (lane == tile) | ((lane == TILES) & absent), 1.0, 0.0
        ).astype(BF)
    value_s[:, HD:] = jnp.ones((SLOTS, HD), BF)
    query_ext = jnp.concatenate([q_ref[:, WIDTH:], far_ref[:, WIDTH:]], axis=0)
    wide = lax.broadcasted_iota(jnp.int32, (2 * ROWS, HD), 1)
    totals = jnp.zeros((2 * ROWS, HD), F32)
    for head in range(HEADS):
        columns = slice(head * HD, (head + 1) * HD)
        query = jnp.concatenate([q_ref[:, columns], far_ref[:, columns]], axis=0)
        scores = lax.dot_general(
            jnp.concatenate([query, query_ext], axis=1),
            key_s[...],
            (((1,), (1,)), ((), ())),
            preferred_element_type=F32,
        )
        weights = jnp.exp2(scores * (math.log2(math.e) / math.sqrt(HD))).astype(BF)
        result = jnp.dot(weights, value_s[...], preferred_element_type=F32)
        numer = result[:, :HD].astype(BF)
        o_ref[ylo, :, columns] = numer[:ROWS]
        o_ref[1 - ylo, :, columns] = numer[ROWS:]
        totals = jnp.where(wide % HEADS == head, result[:, HD:], totals)
    high = totals.astype(BF)
    low = (totals - high.astype(F32)).astype(BF)
    packed = jnp.where(wide < HEADS, high.astype(F32), low.astype(F32)).astype(BF)
    o_ref[ylo, :, WIDTH:] = packed[:ROWS]
    o_ref[1 - ylo, :, WIDTH:] = packed[ROWS:]


def attend(place, query, far, k_gain, mine, theirs):
    return pl.pallas_call(
        attend_kernel,
        in_specs=[smem(), vmem(), vmem(), vmem(), vmem(), vmem()],
        out_specs=vmem(),
        out_shape=jax.ShapeDtypeStruct((2, ROWS, WIDTH + HD), BF),
        scratch_shapes=[pltpu.VMEM((SLOTS, 2 * HD), BF), pltpu.VMEM((SLOTS, 2 * HD), BF)],
        compiler_params=params(32),
        name="attend",
    )(place, query, far, k_gain.reshape(1, HD), mine, theirs)


def combine_kernel(near_ref, far_ref, o_ref):
    for block in range(2):
        summed = near_ref[block].astype(F32) + far_ref[block].astype(F32)
        for head in range(HEADS):
            columns = slice(head * HD, (head + 1) * HD)
            high = summed[:, WIDTH + head : WIDTH + head + 1]
            low = summed[:, WIDTH + HEADS + head : WIDTH + HEADS + head + 1]
            rows = slice(block * ROWS, (block + 1) * ROWS)
            o_ref[rows, columns] = (summed[:, columns] / (high + low)).astype(BF)


def combine(near, far):
    return pl.pallas_call(
        combine_kernel,
        in_specs=[vmem(), vmem()],
        out_specs=vmem(),
        out_shape=jax.ShapeDtypeStruct((2 * ROWS, WIDTH), BF),
        compiler_params=params(4),
        name="combine",
    )(near, far)


def reduce_kernel(x_ref, o_ref):
    for core in range(2):
        for side in range(2):
            total = jnp.zeros((HD, ROWS), F32)
            for source in range(16):
                if source // 2 % 2 == core:
                    total = total + x_ref[source, side].astype(F32)
            begin = (2 * side + core) * HD
            o_ref[:, begin : begin + HD] = total.T.astype(BF)


def reduce(parts):
    return pl.pallas_call(
        reduce_kernel,
        in_specs=[vmem()],
        out_specs=vmem(),
        out_shape=jax.ShapeDtypeStruct((ROWS, WIDTH), BF),
        compiler_params=params(4),
        name="reduce",
    )(parts)


def local(queries, vision, kv_weight, out_weight, q_gain, k_gain, tile_counts, spans):
    core = lax.axis_index("core")
    ylo = lax.axis_index("ylo")

    place = jnp.concatenate([jnp.stack([core, ylo]).astype(jnp.int32), tile_counts])

    query = prepare(queries, q_gain, spans)

    kept = lax.dynamic_slice_in_dim(out_weight, core * HD, HD, axis=1)
    sent = lax.dynamic_slice_in_dim(out_weight, (1 - core) * HD, HD, axis=1)
    got, query = lax.optimization_barrier((swapped(sent, "core"), query))
    pair = jnp.concatenate([kept, got], axis=0)
    far = swapped(query, "ylo")
    weight = lax.all_gather(pair, "z", axis=0, tiled=False)

    both = jnp.transpose(kv_weight, (0, 2, 1)).reshape(HD, vision.shape[1])
    projected = lax.dot_general(
        vision, both, (((1,), (1,)), ((), ())), preferred_element_type=F32
    ).astype(BF)
    projected, far = lax.optimization_barrier((projected, far))
    mine = lax.all_gather(projected, "z", axis=0, tiled=False)
    theirs = swapped(mine, "core")

    partial = attend(place, query, far, k_gain, mine, theirs)
    own = combine(partial, swapped(partial, "ylo"))
    other = swapped(own, "core")

    attended = jnp.concatenate([own, other], axis=1).reshape(2, ROWS, 2 * WIDTH)
    split = weight.reshape(8, 2, 2 * WIDTH, HD)
    product = jnp.einsum("rmk,jtkn->jrtnm", attended, split, preferred_element_type=F32)
    product = product.astype(BF).reshape(16, 2, HD, ROWS)
    parts = lax.all_to_all(product, ("xl", "yhi", "core", "xh"), 0, 0, tiled=True)
    return placed(reduce(parts))


def solution(mesh):
    split = Mesh(mesh.devices.reshape(SIZES), AXES)
    seq, head = ("ylo", "z"), ("xh", "xl", "yhi", "core")
    return jax.shard_map(
        local,
        mesh=split,
        in_specs=(
            P(seq, head),
            P(seq, None),
            P(None, None, head),
            P(head, seq),
            P(),
            P(),
            P(),
            P(seq, None),
        ),
        out_specs=P(seq, head),
        check_vma=False,
    )
```

```python
import math

import jax
import jax.numpy as jnp
from jax import lax
from jax.experimental import pallas as pl
from jax.experimental.pallas import tpu as pltpu
from jax.sharding import Mesh, PartitionSpec as P

HD = 128
TILES = 4
EPSILON = 1e-05
NEG = -1e30
AXES = ("ylo", "z", "xh", "xl", "yhi", "core")
SIZES = (2, 16, 2, 2, 2, 2)
ROWS = 128
FULL = ROWS + 8
HEADS = 4
WIDTH = HEADS * HD
LOCAL = 200
BLOCKS = 16
SLOTS = BLOCKS * LOCAL
BF = jnp.bfloat16
F32 = jnp.float32


def flat(ylo, z, x, yhi, core):
    return (((ylo * 16 + z) * 4 + x) * 2 + yhi) * 2 + core


def swapped(value, axis):
    return lax.ppermute(value, axis, [(0, 1), (1, 0)])


def placed(value):
    pairs = []
    for source in range(512):
        core, yhi, x, z = source % 2, source // 2 % 2, source // 4 % 4, source // 16 % 16
        target = flat(x // 2, z, 2 * (source // 256) + x % 2, yhi, core)
        pairs.append((source, target))
    return lax.ppermute(value, AXES, pairs)


def vmem():
    return pl.BlockSpec(memory_space=pltpu.VMEM)


def smem():
    return pl.BlockSpec(memory_space=pltpu.SMEM)


def params(mib):
    return pltpu.CompilerParams(vmem_limit_bytes=mib << 20)


def prepare_kernel(q_ref, gain_ref, span_ref, o_ref):
    gain = gain_ref[...]
    for head in range(HEADS):
        columns = slice(head * HD, (head + 1) * HD)
        field = q_ref[:, columns].astype(F32)
        mean_sq = jnp.mean(field * field, axis=1, keepdims=True)
        o_ref[:ROWS, columns] = (field / jnp.sqrt(mean_sq + EPSILON) * gain).astype(BF)
    o_ref[ROWS:, :] = jnp.zeros((8, WIDTH), BF)
    o_ref[ROWS:, :HD] = jnp.concatenate(
        [span_ref[...].astype(F32), jnp.zeros((6, HD), F32)], axis=0
    ).astype(BF)


def prepare(queries, q_gain, spans):
    inputs = (queries, q_gain.reshape(1, HD), spans.T)
    return pl.pallas_call(
        prepare_kernel,
        grid=(1,),
        in_specs=[pl.BlockSpec(value.shape, lambda i: (0, 0)) for value in inputs],
        out_specs=pl.BlockSpec((FULL, WIDTH), lambda i: (0, 0)),
        out_shape=jax.ShapeDtypeStruct((FULL, WIDTH), BF),
        compiler_params=params(4),
        name="prepare",
    )(*(pltpu.with_memory_space_constraint(value, pltpu.HBM) for value in inputs))


def column(row, count):
    width = row.shape[1]
    across = lax.broadcasted_iota(jnp.int32, (count, width), 1)
    down = lax.broadcasted_iota(jnp.int32, (count, width), 0)
    return jnp.sum(jnp.where(across == down, row, 0.0), axis=1, keepdims=True)


def pack_kernel(place_ref, x_ref, own_ref, other_ref, gain_ref, o_ref):
    mean_sq = (column(own_ref[...], LOCAL) + column(other_ref[...], LOCAL)) / HD
    gain = gain_ref[...]
    gain = jnp.where(place_ref[0] == 0, gain, jnp.concatenate([gain[:, HD // 2 :]] * 2, axis=1))
    lane = lax.broadcasted_iota(jnp.int32, (LOCAL, HD), 1)
    field = x_ref[...]
    key = field / jnp.sqrt(mean_sq + EPSILON) * gain
    o_ref[...] = jnp.where(lane < HD // 2, key, field).astype(BF)


def pack(place, projected, own_squares, other_squares, k_gain):
    return pl.pallas_call(
        pack_kernel,
        in_specs=[smem(), vmem(), vmem(), vmem(), vmem()],
        out_specs=vmem(),
        out_shape=jax.ShapeDtypeStruct((LOCAL, HD), BF),
        compiler_params=params(4),
        name="pack",
    )(
        place,
        projected,
        own_squares.reshape(1, LOCAL),
        other_squares.reshape(1, LOCAL),
        k_gain.reshape(1, HD),
    )


def masked(rows):
    rows = rows.astype(F32)
    begin, end = column(rows[0:1], ROWS), column(rows[1:2], ROWS)
    lane = lax.broadcasted_iota(jnp.int32, (ROWS, HD), 1)
    place = lane.astype(F32)
    inside = (begin <= place) & (place < end)
    return jnp.where((lane <= TILES) & ~inside, NEG, 0.0).astype(BF)


def attend_kernel(place_ref, q_ref, far_ref, mine_ref, theirs_ref, o_ref, key_s, value_s):
    core, ylo = place_ref[0], place_ref[1]
    half = HD // 2
    lane = lax.broadcasted_iota(jnp.int32, (LOCAL, HD), 1)
    item = lax.broadcasted_iota(jnp.int32, (LOCAL, HD), 0)
    for block in range(BLOCKS):
        rows = slice(block * LOCAL, (block + 1) * LOCAL)
        mine, theirs = mine_ref[block], theirs_ref[block]
        left = jnp.where(core == 0, mine, theirs)
        right = jnp.where(core == 0, theirs, mine)
        key_s[rows, :HD] = jnp.concatenate([left[:, :half], right[:, :half]], axis=1)
        value_s[rows, :HD] = jnp.concatenate([left[:, half:], right[:, half:]], axis=1)
        tile = 2 * ylo + block // 8
        absent = item + (block % 8) * LOCAL >= place_ref[2 + tile]
        key_s[rows, HD:] = jnp.where(
            (lane == tile) | ((lane == TILES) & absent), 1.0, 0.0
        ).astype(BF)
    value_s[:, HD:] = jnp.ones((SLOTS, HD), BF)
    query_ext = jnp.concatenate([masked(q_ref[ROWS:, :HD]), masked(far_ref[ROWS:, :HD])], axis=0)
    wide = lax.broadcasted_iota(jnp.int32, (2 * ROWS, HD), 1)
    totals = jnp.zeros((2 * ROWS, HD), F32)
    for head in range(HEADS):
        columns = slice(head * HD, (head + 1) * HD)
        query = jnp.concatenate([q_ref[:ROWS, columns], far_ref[:ROWS, columns]], axis=0)
        scores = lax.dot_general(
            jnp.concatenate([query, query_ext], axis=1),
            key_s[...],
            (((1,), (1,)), ((), ())),
            preferred_element_type=F32,
        )
        weights = jnp.exp2(scores * (math.log2(math.e) / math.sqrt(HD))).astype(BF)
        result = jnp.dot(weights, value_s[...], preferred_element_type=F32)
        numer = result[:, :HD].astype(BF)
        o_ref[ylo, :ROWS, columns] = numer[:ROWS]
        o_ref[1 - ylo, :ROWS, columns] = numer[ROWS:]
        totals = jnp.where(wide % HEADS == head, result[:, HD:], totals)
    sums = totals.T[:8]
    high = sums.astype(BF).astype(F32)
    part = lax.broadcasted_iota(jnp.int32, (8, 2 * ROWS), 0)
    packed = jnp.where(part < HEADS, high, sums - high).astype(BF)
    empty = jnp.zeros((8, WIDTH), BF)
    o_ref[ylo, ROWS:, :] = empty
    o_ref[1 - ylo, ROWS:, :] = empty
    o_ref[ylo, ROWS:, :HD] = packed[:, :ROWS]
    o_ref[1 - ylo, ROWS:, :HD] = packed[:, ROWS:]


def attend(place, query, far, mine, theirs):
    return pl.pallas_call(
        attend_kernel,
        in_specs=[smem(), vmem(), vmem(), vmem(), vmem()],
        out_specs=vmem(),
        out_shape=jax.ShapeDtypeStruct((2, FULL, WIDTH), BF),
        scratch_shapes=[pltpu.VMEM((SLOTS, 2 * HD), BF), pltpu.VMEM((SLOTS, 2 * HD), BF)],
        compiler_params=params(32),
        name="attend",
    )(place, query, far, mine, theirs)


def combine_kernel(near_ref, far_ref, o_ref):
    for block in range(2):
        totals = near_ref[block, ROWS:, :HD].astype(F32) + far_ref[block, ROWS:, :HD].astype(F32)
        totals = totals[:HEADS] + totals[HEADS:]
        rows = slice(block * ROWS, (block + 1) * ROWS)
        for head in range(HEADS):
            columns = slice(head * HD, (head + 1) * HD)
            summed = near_ref[block, :ROWS, columns].astype(F32)
            summed = summed + far_ref[block, :ROWS, columns].astype(F32)
            total = column(totals[head : head + 1], ROWS)
            o_ref[rows, columns] = (summed / total).astype(BF)


def combine(near, far):
    return pl.pallas_call(
        combine_kernel,
        in_specs=[vmem(), vmem()],
        out_specs=vmem(),
        out_shape=jax.ShapeDtypeStruct((2 * ROWS, WIDTH), BF),
        compiler_params=params(4),
        name="combine",
    )(near, far)


def reduce_kernel(x_ref, o_ref):
    for core in range(2):
        for side in range(2):
            total = jnp.zeros((HD, ROWS), F32)
            for source in range(16):
                if source // 2 % 2 == core:
                    total = total + x_ref[source, side].astype(F32)
            begin = (2 * side + core) * HD
            o_ref[:, begin : begin + HD] = total.T.astype(BF)


def reduce(parts):
    return pl.pallas_call(
        reduce_kernel,
        in_specs=[vmem()],
        out_specs=vmem(),
        out_shape=jax.ShapeDtypeStruct((ROWS, WIDTH), BF),
        compiler_params=params(4),
        name="reduce",
    )(parts)


def local(queries, vision, kv_weight, out_weight, q_gain, k_gain, tile_counts, spans):
    core = lax.axis_index("core")
    ylo = lax.axis_index("ylo")
    half = HD // 2

    place = jnp.concatenate([jnp.stack([core, ylo]).astype(jnp.int32), tile_counts])

    query = prepare(queries, q_gain, spans)

    kept = lax.dynamic_slice_in_dim(out_weight, core * HD, HD, axis=1)
    sent = lax.dynamic_slice_in_dim(out_weight, (1 - core) * HD, HD, axis=1)
    got, query = lax.optimization_barrier((swapped(sent, "core"), query))
    pair = jnp.concatenate([kept, got], axis=0)
    far = swapped(query, "ylo")
    weight = lax.all_gather(pair, "z", axis=0, tiled=False)

    both = jnp.transpose(kv_weight, (0, 2, 1)).reshape(HD, vision.shape[1])
    projected = lax.dot_general(
        vision, both, (((1,), (1,)), ((), ())), preferred_element_type=F32
    )
    projected, far = lax.optimization_barrier((projected, far))
    key_raw = projected[:, :half]
    own_squares = jnp.sum(key_raw * key_raw, axis=1)
    local_pair = pack(place, projected, own_squares, swapped(own_squares, "core"), k_gain)
    mine = lax.all_gather(local_pair, "z", axis=0, tiled=False)
    theirs = swapped(mine, "core")

    partial = attend(place, query, far, mine, theirs)
    own = combine(partial, swapped(partial, "ylo"))
    other = swapped(own, "core")

    attended = jnp.concatenate([own, other], axis=1).reshape(2, ROWS, 2 * WIDTH)
    split = weight.reshape(8, 2, 2 * WIDTH, HD)
    product = jnp.einsum("rmk,jtkn->jrtnm", attended, split, preferred_element_type=F32)
    product = product.astype(BF).reshape(16, 2, HD, ROWS)
    parts = lax.all_to_all(product, ("xl", "yhi", "core", "xh"), 0, 0, tiled=True)
    return placed(reduce(parts))


def solution(mesh):
    split = Mesh(mesh.devices.reshape(SIZES), AXES)
    seq, head = ("ylo", "z"), ("xh", "xl", "yhi", "core")
    return jax.shard_map(
        local,
        mesh=split,
        in_specs=(
            P(seq, head),
            P(seq, None),
            P(None, None, head),
            P(head, seq),
            P(),
            P(),
            P(),
            P(seq, None),
        ),
        out_specs=P(seq, head),
        check_vma=False,
    )
```

```python
import math

import jax
import jax.numpy as jnp
from jax import lax
from jax.experimental import pallas as pl
from jax.experimental.pallas import tpu as pltpu
from jax.sharding import Mesh, PartitionSpec as P

HD = 128
TILES = 4
EPSILON = 1e-05
NEG = -1e30
AXES = ("ylo", "z", "xh", "xl", "yhi", "core")
SIZES = (2, 16, 2, 2, 2, 2)
ROWS = 128
FULL = ROWS + 8
HEADS = 4
WIDTH = HEADS * HD
LOCAL = 200
BLOCKS = 16
SLOTS = BLOCKS * LOCAL
BF = jnp.bfloat16
F32 = jnp.float32


def flat(ylo, z, x, yhi, core):
    return (((ylo * 16 + z) * 4 + x) * 2 + yhi) * 2 + core


def swapped(value, axis):
    return lax.ppermute(value, axis, [(0, 1), (1, 0)])


def placed(value):
    pairs = []
    for source in range(512):
        core, yhi, x, z = source % 2, source // 2 % 2, source // 4 % 4, source // 16 % 16
        target = flat(x // 2, z, 2 * (source // 256) + x % 2, yhi, core)
        pairs.append((source, target))
    return lax.ppermute(value, AXES, pairs)


def vmem():
    return pl.BlockSpec(memory_space=pltpu.VMEM)


def smem():
    return pl.BlockSpec(memory_space=pltpu.SMEM)


def params(mib):
    return pltpu.CompilerParams(vmem_limit_bytes=mib << 20)


def prepare_kernel(q_ref, gain_ref, span_ref, o_ref):
    gain = gain_ref[...]
    for head in range(HEADS):
        columns = slice(head * HD, (head + 1) * HD)
        field = q_ref[:, columns].astype(F32)
        mean_sq = jnp.mean(field * field, axis=1, keepdims=True)
        o_ref[:ROWS, columns] = (field / jnp.sqrt(mean_sq + EPSILON) * gain).astype(BF)
    o_ref[ROWS:, :] = jnp.zeros((8, WIDTH), BF)
    o_ref[ROWS:, :HD] = jnp.concatenate(
        [span_ref[...].astype(F32), jnp.zeros((6, HD), F32)], axis=0
    ).astype(BF)


def prepare(queries, q_gain, spans):
    inputs = (queries, q_gain.reshape(1, HD), spans.T)
    return pl.pallas_call(
        prepare_kernel,
        grid=(1,),
        in_specs=[pl.BlockSpec(value.shape, lambda i: (0, 0)) for value in inputs],
        out_specs=pl.BlockSpec((FULL, WIDTH), lambda i: (0, 0)),
        out_shape=jax.ShapeDtypeStruct((FULL, WIDTH), BF),
        compiler_params=params(4),
        name="prepare",
    )(*(pltpu.with_memory_space_constraint(value, pltpu.HBM) for value in inputs))


def column(row, count):
    width = row.shape[1]
    across = lax.broadcasted_iota(jnp.int32, (count, width), 1)
    down = lax.broadcasted_iota(jnp.int32, (count, width), 0)
    return jnp.sum(jnp.where(across == down, row, 0.0), axis=1, keepdims=True)


def pack_kernel(place_ref, x_ref, own_ref, other_ref, gain_ref, o_ref):
    mean_sq = (column(own_ref[...], LOCAL) + column(other_ref[...], LOCAL)) / HD
    gain = gain_ref[...]
    gain = jnp.where(place_ref[0] == 0, gain, jnp.concatenate([gain[:, HD // 2 :]] * 2, axis=1))
    lane = lax.broadcasted_iota(jnp.int32, (LOCAL, HD), 1)
    field = x_ref[...]
    key = field / jnp.sqrt(mean_sq + EPSILON) * gain
    o_ref[...] = jnp.where(lane < HD // 2, key, field).astype(BF)


def pack(place, projected, own_squares, other_squares, k_gain):
    return pl.pallas_call(
        pack_kernel,
        in_specs=[smem(), vmem(), vmem(), vmem(), vmem()],
        out_specs=vmem(),
        out_shape=jax.ShapeDtypeStruct((LOCAL, HD), BF),
        compiler_params=params(4),
        name="pack",
    )(
        place,
        projected,
        own_squares.reshape(1, LOCAL),
        other_squares.reshape(1, LOCAL),
        k_gain.reshape(1, HD),
    )


def masked(rows):
    rows = rows.astype(F32)
    begin, end = column(rows[0:1], ROWS), column(rows[1:2], ROWS)
    lane = lax.broadcasted_iota(jnp.int32, (ROWS, HD), 1)
    place = lane.astype(F32)
    inside = (begin <= place) & (place < end)
    return jnp.where((lane <= TILES) & ~inside, NEG, 0.0).astype(BF)


def attend_kernel(place_ref, q_ref, far_ref, mine_ref, theirs_ref, o_ref, key_s, value_s):
    core, ylo = place_ref[0], place_ref[1]
    half = HD // 2
    lane = lax.broadcasted_iota(jnp.int32, (LOCAL, HD), 1)
    item = lax.broadcasted_iota(jnp.int32, (LOCAL, HD), 0)
    for block in range(BLOCKS):
        rows = slice(block * LOCAL, (block + 1) * LOCAL)
        mine, theirs = mine_ref[block], theirs_ref[block]
        left = jnp.where(core == 0, mine, theirs)
        right = jnp.where(core == 0, theirs, mine)
        key_s[rows, :HD] = jnp.concatenate([left[:, :half], right[:, :half]], axis=1)
        value_s[rows, :HD] = jnp.concatenate([left[:, half:], right[:, half:]], axis=1)
        tile = 2 * ylo + block // 8
        absent = item + (block % 8) * LOCAL >= place_ref[2 + tile]
        key_s[rows, HD:] = jnp.where(
            (lane == tile) | ((lane == TILES) & absent), 1.0, 0.0
        ).astype(BF)
    value_s[:, HD:] = jnp.ones((SLOTS, HD), BF)
    query_ext = jnp.concatenate([masked(q_ref[ROWS:, :HD]), masked(far_ref[ROWS:, :HD])], axis=0)
    wide = lax.broadcasted_iota(jnp.int32, (2 * ROWS, HD), 1)
    totals = jnp.zeros((2 * ROWS, HD), F32)
    for head in range(HEADS):
        columns = slice(head * HD, (head + 1) * HD)
        query = jnp.concatenate([q_ref[:ROWS, columns], far_ref[:ROWS, columns]], axis=0)
        scores = lax.dot_general(
            jnp.concatenate([query, query_ext], axis=1),
            key_s[...],
            (((1,), (1,)), ((), ())),
            preferred_element_type=F32,
        )
        weights = jnp.exp2(scores * (math.log2(math.e) / math.sqrt(HD))).astype(BF)
        result = jnp.dot(weights, value_s[...], preferred_element_type=F32)
        numer = result[:, :HD].astype(BF)
        o_ref[ylo, :ROWS, columns] = numer[:ROWS]
        o_ref[1 - ylo, :ROWS, columns] = numer[ROWS:]
        totals = jnp.where(wide % HEADS == head, result[:, HD:], totals)
    sums = totals.T[:8]
    high = sums.astype(BF).astype(F32)
    part = lax.broadcasted_iota(jnp.int32, (8, 2 * ROWS), 0)
    packed = jnp.where(part < HEADS, high, sums - high).astype(BF)
    empty = jnp.zeros((8, WIDTH), BF)
    o_ref[ylo, ROWS:, :] = empty
    o_ref[1 - ylo, ROWS:, :] = empty
    o_ref[ylo, ROWS:, :HD] = packed[:, :ROWS]
    o_ref[1 - ylo, ROWS:, :HD] = packed[:, ROWS:]


def attend(place, query, far, mine, theirs):
    return pl.pallas_call(
        attend_kernel,
        in_specs=[smem(), vmem(), vmem(), vmem(), vmem()],
        out_specs=vmem(),
        out_shape=jax.ShapeDtypeStruct((2, FULL, WIDTH), BF),
        scratch_shapes=[pltpu.VMEM((SLOTS, 2 * HD), BF), pltpu.VMEM((SLOTS, 2 * HD), BF)],
        compiler_params=params(32),
        name="attend",
    )(place, query, far, mine, theirs)


def combine_kernel(near_ref, far_ref, o_ref):
    for block in range(2):
        totals = near_ref[block, ROWS:, :HD].astype(F32) + far_ref[block, ROWS:, :HD].astype(F32)
        totals = totals[:HEADS] + totals[HEADS:]
        rows = slice(block * ROWS, (block + 1) * ROWS)
        for head in range(HEADS):
            columns = slice(head * HD, (head + 1) * HD)
            summed = near_ref[block, :ROWS, columns].astype(F32)
            summed = summed + far_ref[block, :ROWS, columns].astype(F32)
            total = column(totals[head : head + 1], ROWS)
            o_ref[rows, columns] = (summed / total).astype(BF)


def combine(near, far):
    return pl.pallas_call(
        combine_kernel,
        in_specs=[vmem(), vmem()],
        out_specs=vmem(),
        out_shape=jax.ShapeDtypeStruct((2 * ROWS, WIDTH), BF),
        compiler_params=params(4),
        name="combine",
    )(near, far)


def merge_kernel(core_ref, own_ref, got_ref, o_ref, sem):
    begin = pl.multiple_of(core_ref[0] * HD, HD)
    copies = []
    for index, source in enumerate((own_ref, got_ref)):
        copy = pltpu.make_async_copy(
            source.at[:, pl.ds(begin, HD)], o_ref.at[pl.ds(index * WIDTH, WIDTH)], sem.at[index]
        )
        copy.start()
        copies.append(copy)
    for copy in copies:
        copy.wait()


def merge(place, own, got):
    hbm = pl.BlockSpec(memory_space=pltpu.HBM)
    return pl.pallas_call(
        merge_kernel,
        in_specs=[smem(), hbm, hbm],
        out_specs=hbm,
        out_shape=jax.ShapeDtypeStruct((2 * WIDTH, HD), BF),
        scratch_shapes=[pltpu.SemaphoreType.DMA((2,))],
        compiler_params=params(4),
        name="merge",
    )(
        place,
        pltpu.with_memory_space_constraint(own, pltpu.HBM),
        pltpu.with_memory_space_constraint(got, pltpu.HBM),
    )


def reduce_kernel(x_ref, o_ref):
    for core in range(2):
        for side in range(2):
            total = jnp.zeros((HD, ROWS), F32)
            for source in range(16):
                if source // 2 % 2 == core:
                    total = total + x_ref[source, side].astype(F32)
            begin = (2 * side + core) * HD
            o_ref[:, begin : begin + HD] = total.T.astype(BF)


def reduce(parts):
    return pl.pallas_call(
        reduce_kernel,
        in_specs=[vmem()],
        out_specs=vmem(),
        out_shape=jax.ShapeDtypeStruct((ROWS, WIDTH), BF),
        compiler_params=params(4),
        name="reduce",
    )(parts)


def local(queries, vision, kv_weight, out_weight, q_gain, k_gain, tile_counts, spans):
    core = lax.axis_index("core")
    ylo = lax.axis_index("ylo")
    half = HD // 2

    place = jnp.concatenate([jnp.stack([core, ylo]).astype(jnp.int32), tile_counts])

    query = prepare(queries, q_gain, spans)

    got, query = lax.optimization_barrier((swapped(out_weight, "core"), query))
    pair = merge(jnp.reshape(core, (1,)).astype(jnp.int32), out_weight, got)
    far = swapped(query, "ylo")
    weight = lax.all_gather(pair, "z", axis=0, tiled=False)

    both = jnp.transpose(kv_weight, (0, 2, 1)).reshape(HD, vision.shape[1])
    projected = lax.dot_general(
        vision, both, (((1,), (1,)), ((), ())), preferred_element_type=F32
    )
    projected, far = lax.optimization_barrier((projected, far))
    key_raw = projected[:, :half]
    own_squares = jnp.sum(key_raw * key_raw, axis=1)
    local_pair = pack(place, projected, own_squares, swapped(own_squares, "core"), k_gain)
    mine = lax.all_gather(local_pair, "z", axis=0, tiled=False)
    theirs = swapped(mine, "core")

    partial = attend(place, query, far, mine, theirs)
    own = combine(partial, swapped(partial, "ylo"))
    other = swapped(own, "core")

    attended = jnp.concatenate([own, other], axis=1).reshape(2, ROWS, 2 * WIDTH)
    split = weight.reshape(8, 2, 2 * WIDTH, HD)
    product = jnp.einsum("rmk,jtkn->jrtnm", attended, split, preferred_element_type=F32)
    product = product.astype(BF).reshape(16, 2, HD, ROWS)
    parts = lax.all_to_all(product, ("xl", "yhi", "core", "xh"), 0, 0, tiled=True)
    return placed(reduce(parts))


def solution(mesh):
    split = Mesh(mesh.devices.reshape(SIZES), AXES)
    seq, head = ("ylo", "z"), ("xh", "xl", "yhi", "core")
    return jax.shard_map(
        local,
        mesh=split,
        in_specs=(
            P(seq, head),
            P(seq, None),
            P(None, None, head),
            P(head, seq),
            P(),
            P(),
            P(),
            P(seq, None),
        ),
        out_specs=P(seq, head),
        check_vma=False,
    )
```

```python
import math

import jax
import jax.numpy as jnp
from jax import lax
from jax.experimental import pallas as pl
from jax.experimental.pallas import tpu as pltpu
from jax.sharding import Mesh, PartitionSpec as P

HD = 128
TILES = 4
EPSILON = 1e-05
NEG = -1e30
AXES = ("ylo", "z", "x", "yhi", "core")
SIZES = (2, 16, 4, 2, 2)
ROWS = 128
HEADS = 4
WIDTH = HEADS * HD
LOCAL = 200
BLOCKS = 16
SLOTS = BLOCKS * LOCAL
BF = jnp.bfloat16
F32 = jnp.float32


def flat(ylo, z, x, yhi, core):
    return (((ylo * 16 + z) * 4 + x) * 2 + yhi) * 2 + core


def swapped(value, axis):
    return lax.ppermute(value, axis, [(0, 1), (1, 0)])


def placed(value):
    pairs = []
    for source in range(512):
        core, yhi, x, z = source % 2, source // 2 % 2, source // 4 % 4, source // 16 % 16
        target = flat(x // 2, z, 2 * (source // 256) + x % 2, yhi, core)
        pairs.append((source, target))
    return lax.ppermute(value, AXES, pairs)


def vmem():
    return pl.BlockSpec(memory_space=pltpu.VMEM)


def smem():
    return pl.BlockSpec(memory_space=pltpu.SMEM)


def params(mib):
    return pltpu.CompilerParams(vmem_limit_bytes=mib << 20)


def prepare_kernel(q_ref, gain_ref, span_ref, o_ref):
    gain = gain_ref[...]
    for head in range(HEADS):
        columns = slice(head * HD, (head + 1) * HD)
        field = q_ref[:, columns].astype(F32)
        mean_sq = jnp.mean(field * field, axis=1, keepdims=True)
        o_ref[:, columns] = (field / jnp.sqrt(mean_sq + EPSILON) * gain).astype(BF)
    row = lax.broadcasted_iota(jnp.int32, (ROWS, HD), 0)
    lane = lax.broadcasted_iota(jnp.int32, (ROWS, HD), 1)
    begin = jnp.sum(jnp.where(row == lane, span_ref[0:1, :], 0), axis=1, keepdims=True)
    end = jnp.sum(jnp.where(row == lane, span_ref[1:2, :], 0), axis=1, keepdims=True)
    inside = (begin <= lane) & (lane < end)
    o_ref[:, WIDTH:] = jnp.where((lane <= TILES) & ~inside, NEG, 0.0).astype(BF)


def prepare(queries, q_gain, spans):
    inputs = (queries, q_gain.reshape(1, HD), spans.T)
    return pl.pallas_call(
        prepare_kernel,
        grid=(1,),
        in_specs=[pl.BlockSpec(value.shape, lambda i: (0, 0)) for value in inputs],
        out_specs=pl.BlockSpec((ROWS, WIDTH + HD), lambda i: (0, 0)),
        out_shape=jax.ShapeDtypeStruct((ROWS, WIDTH + HD), BF),
        compiler_params=params(4),
        name="prepare",
    )(*(pltpu.with_memory_space_constraint(value, pltpu.HBM) for value in inputs))


def column(row, count):
    width = row.shape[1]
    across = lax.broadcasted_iota(jnp.int32, (count, width), 1)
    down = lax.broadcasted_iota(jnp.int32, (count, width), 0)
    return jnp.sum(jnp.where(across == down, row, 0.0), axis=1, keepdims=True)


def pack_kernel(place_ref, x_ref, own_ref, other_ref, gain_ref, o_ref):
    mean_sq = (column(own_ref[...], LOCAL) + column(other_ref[...], LOCAL)) / HD
    gain = gain_ref[...]
    gain = jnp.where(place_ref[0] == 0, gain, jnp.concatenate([gain[:, HD // 2 :]] * 2, axis=1))
    lane = lax.broadcasted_iota(jnp.int32, (LOCAL, HD), 1)
    field = x_ref[...]
    key = field / jnp.sqrt(mean_sq + EPSILON) * gain
    o_ref[...] = jnp.where(lane < HD // 2, key, field).astype(BF)


def pack(place, projected, own_squares, other_squares, k_gain):
    return pl.pallas_call(
        pack_kernel,
        in_specs=[smem(), vmem(), vmem(), vmem(), vmem()],
        out_specs=vmem(),
        out_shape=jax.ShapeDtypeStruct((LOCAL, HD), BF),
        compiler_params=params(4),
        name="pack",
    )(
        place,
        projected,
        own_squares.reshape(1, LOCAL),
        other_squares.reshape(1, LOCAL),
        k_gain.reshape(1, HD),
    )


def attend_kernel(place_ref, q_ref, far_ref, mine_ref, theirs_ref, o_ref, key_s, value_s):
    core, ylo = place_ref[0], place_ref[1]
    half = HD // 2
    lane = lax.broadcasted_iota(jnp.int32, (LOCAL, HD), 1)
    item = lax.broadcasted_iota(jnp.int32, (LOCAL, HD), 0)
    for block in range(BLOCKS):
        rows = slice(block * LOCAL, (block + 1) * LOCAL)
        mine, theirs = mine_ref[block], theirs_ref[block]
        left = jnp.where(core == 0, mine, theirs)
        right = jnp.where(core == 0, theirs, mine)
        key_s[rows, :HD] = jnp.concatenate([left[:, :half], right[:, :half]], axis=1)
        value_s[rows, :HD] = jnp.concatenate([left[:, half:], right[:, half:]], axis=1)
        tile = 2 * ylo + block // 8
        absent = item + (block % 8) * LOCAL >= place_ref[2 + tile]
        key_s[rows, HD:] = jnp.where(
            (lane == tile) | ((lane == TILES) & absent), 1.0, 0.0
        ).astype(BF)
    value_s[:, HD:] = jnp.ones((SLOTS, HD), BF)
    query_ext = jnp.concatenate([q_ref[:, WIDTH:], far_ref[:, WIDTH:]], axis=0)
    wide = lax.broadcasted_iota(jnp.int32, (2 * ROWS, HD), 1)
    totals = jnp.zeros((2 * ROWS, HD), F32)
    for head in range(HEADS):
        columns = slice(head * HD, (head + 1) * HD)
        query = jnp.concatenate([q_ref[:, columns], far_ref[:, columns]], axis=0)
        scores = lax.dot_general(
            jnp.concatenate([query, query_ext], axis=1),
            key_s[...],
            (((1,), (1,)), ((), ())),
            preferred_element_type=F32,
        )
        weights = jnp.exp2(scores * (math.log2(math.e) / math.sqrt(HD))).astype(BF)
        result = jnp.dot(weights, value_s[...], preferred_element_type=F32)
        numer = result[:, :HD].astype(BF)
        o_ref[ylo, :, columns] = numer[:ROWS]
        o_ref[1 - ylo, :, columns] = numer[ROWS:]
        totals = jnp.where(wide % HEADS == head, result[:, HD:], totals)
    high = totals.astype(BF)
    low = (totals - high.astype(F32)).astype(BF)
    packed = jnp.where(wide < HEADS, high.astype(F32), low.astype(F32)).astype(BF)
    o_ref[ylo, :, WIDTH:] = packed[:ROWS]
    o_ref[1 - ylo, :, WIDTH:] = packed[ROWS:]


def attend(place, query, far, mine, theirs):
    return pl.pallas_call(
        attend_kernel,
        in_specs=[smem(), vmem(), vmem(), vmem(), vmem()],
        out_specs=vmem(),
        out_shape=jax.ShapeDtypeStruct((2, ROWS, WIDTH + HD), BF),
        scratch_shapes=[pltpu.VMEM((SLOTS, 2 * HD), BF), pltpu.VMEM((SLOTS, 2 * HD), BF)],
        compiler_params=params(32),
        name="attend",
    )(place, query, far, mine, theirs)


def combine_kernel(near_ref, far_ref, o_ref):
    for block in range(2):
        summed = near_ref[block].astype(F32) + far_ref[block].astype(F32)
        for head in range(HEADS):
            columns = slice(head * HD, (head + 1) * HD)
            high = summed[:, WIDTH + head : WIDTH + head + 1]
            low = summed[:, WIDTH + HEADS + head : WIDTH + HEADS + head + 1]
            rows = slice(block * ROWS, (block + 1) * ROWS)
            o_ref[rows, columns] = (summed[:, columns] / (high + low)).astype(BF)


def combine(near, far):
    return pl.pallas_call(
        combine_kernel,
        in_specs=[vmem(), vmem()],
        out_specs=vmem(),
        out_shape=jax.ShapeDtypeStruct((2 * ROWS, WIDTH), BF),
        compiler_params=params(4),
        name="combine",
    )(near, far)


def project_kernel(own_ref, other_hbm, w_hbm, o_ref, a_s, w_s, sem):
    steps = BLOCKS // 4
    other = pltpu.make_async_copy(other_hbm, a_s.at[:, pl.ds(WIDTH, WIDTH)], sem.at[steps])
    other.start()
    for step in range(steps):
        blocks = pl.ds(4 * step, 4)
        pltpu.make_async_copy(w_hbm.at[blocks], w_s.at[blocks], sem.at[step]).start()
    a_s[:, :WIDTH] = own_ref[...]
    other.wait()

    def body(step, carry):
        blocks = pl.ds(4 * step, 4)
        pltpu.make_async_copy(w_hbm.at[blocks], w_s.at[blocks], sem.at[step]).wait()
        for index in range(2):
            block = 4 * step + 2 * index
            weight = jnp.concatenate([w_s[block], w_s[block + 1]], axis=1)
            result = jnp.dot(a_s[...], weight, preferred_element_type=F32).astype(BF)
            o_ref[0, 2 * step + index] = result[:ROWS]
            o_ref[1, 2 * step + index] = result[ROWS:]
        return carry

    lax.fori_loop(0, steps, body, 0)


def project(own, other, weight):
    hbm = pl.BlockSpec(memory_space=pltpu.HBM)
    return pl.pallas_call(
        project_kernel,
        in_specs=[vmem(), hbm, hbm],
        out_specs=vmem(),
        out_shape=jax.ShapeDtypeStruct((2, 8, ROWS, 2 * HD), BF),
        scratch_shapes=[
            pltpu.VMEM((2 * ROWS, 2 * WIDTH), BF),
            pltpu.VMEM((BLOCKS, 2 * WIDTH, HD), BF),
            pltpu.SemaphoreType.DMA((5,)),
        ],
        compiler_params=params(12),
        name="project",
    )(
        own,
        pltpu.with_memory_space_constraint(other, pltpu.HBM),
        pltpu.with_memory_space_constraint(weight, pltpu.HBM),
    )


def reduce_kernel(x_ref, o_ref):
    for core in range(2):
        total = x_ref[core].astype(F32)
        for source in range(1, 8):
            total = total + x_ref[2 * source + core].astype(F32)
        total = total.astype(BF)
        o_ref[:, core * HD : (core + 1) * HD] = total[:, :HD]
        o_ref[:, (2 + core) * HD : (3 + core) * HD] = total[:, HD:]


def reduce(parts):
    return pl.pallas_call(
        reduce_kernel,
        in_specs=[vmem()],
        out_specs=vmem(),
        out_shape=jax.ShapeDtypeStruct((ROWS, WIDTH), BF),
        compiler_params=params(4),
        name="reduce",
    )(parts)


def local(queries, vision, kv_weight, out_weight, q_gain, k_gain, tile_counts, spans):
    core = lax.axis_index("core")
    ylo = lax.axis_index("ylo")
    half = HD // 2

    place = jnp.concatenate([jnp.stack([core, ylo]).astype(jnp.int32), tile_counts])

    query = prepare(queries, q_gain, spans)

    kept = lax.dynamic_slice_in_dim(out_weight, core * HD, HD, axis=1)
    sent = lax.dynamic_slice_in_dim(out_weight, (1 - core) * HD, HD, axis=1)
    got, query = lax.optimization_barrier((swapped(sent, "core"), query))
    pair = jnp.concatenate([kept, got], axis=0)
    far = swapped(query, "ylo")
    weight = lax.all_gather(pair, "z", axis=0, tiled=False)

    both = jnp.transpose(kv_weight, (0, 2, 1)).reshape(HD, vision.shape[1])
    projected = lax.dot_general(
        vision, both, (((1,), (1,)), ((), ())), preferred_element_type=F32
    )
    projected, far = lax.optimization_barrier((projected, far))
    key_raw = projected[:, :half]
    own_squares = jnp.sum(key_raw * key_raw, axis=1)
    local_pair = pack(place, projected, own_squares, swapped(own_squares, "core"), k_gain)
    mine = lax.all_gather(local_pair, "z", axis=0, tiled=False)
    theirs = swapped(mine, "core")

    partial = attend(place, query, far, mine, theirs)
    own = combine(partial, swapped(partial, "ylo"))
    other = swapped(own, "core")

    product = project(own, other, weight).reshape(16, ROWS, 2 * HD)
    parts = lax.all_to_all(product, ("x", "yhi", "core"), 0, 0, tiled=True)
    return placed(reduce(parts))


def solution(mesh):
    split = Mesh(mesh.devices.reshape(SIZES), AXES)
    seq, head = ("ylo", "z"), ("x", "yhi", "core")
    return jax.shard_map(
        local,
        mesh=split,
        in_specs=(
            P(seq, head),
            P(seq, None),
            P(None, None, head),
            P(head, seq),
            P(),
            P(),
            P(),
            P(seq, None),
        ),
        out_specs=P(seq, head),
        check_vma=False,
    )
```

```python
import math

import jax
import jax.numpy as jnp
from jax import lax
from jax.experimental import pallas as pl
from jax.experimental.pallas import tpu as pltpu
from jax.sharding import Mesh, PartitionSpec as P

HD = 128
TILES = 4
EPSILON = 1e-05
NEG = -1e30
AXES = ("ylo", "z", "x", "yhi", "core")
SIZES = (2, 16, 4, 2, 2)
ROWS = 128
HEADS = 4
WIDTH = HEADS * HD
LOCAL = 200
BLOCKS = 16
SLOTS = BLOCKS * LOCAL
BF = jnp.bfloat16
F32 = jnp.float32


def flat(ylo, z, x, yhi, core):
    return (((ylo * 16 + z) * 4 + x) * 2 + yhi) * 2 + core


def swapped(value, axis):
    return lax.ppermute(value, axis, [(0, 1), (1, 0)])


def placed(value):
    pairs = []
    for source in range(512):
        core, yhi, x, z = source % 2, source // 2 % 2, source // 4 % 4, source // 16 % 16
        ylo = source // 256
        stays = x // 2 == ylo
        target = source if stays else flat(1 - ylo, z, 3 - x, yhi, core)
        pairs.append((source, target))
    return lax.ppermute(value, AXES, pairs)


def vmem():
    return pl.BlockSpec(memory_space=pltpu.VMEM)


def smem():
    return pl.BlockSpec(memory_space=pltpu.SMEM)


def params(mib):
    return pltpu.CompilerParams(vmem_limit_bytes=mib << 20)


def prepare_kernel(q_ref, gain_ref, span_ref, o_ref):
    gain = gain_ref[...]
    for head in range(HEADS):
        columns = slice(head * HD, (head + 1) * HD)
        field = q_ref[:, columns].astype(F32)
        mean_sq = jnp.mean(field * field, axis=1, keepdims=True)
        o_ref[:, columns] = (field / jnp.sqrt(mean_sq + EPSILON) * gain).astype(BF)
    row = lax.broadcasted_iota(jnp.int32, (ROWS, HD), 0)
    lane = lax.broadcasted_iota(jnp.int32, (ROWS, HD), 1)
    begin = jnp.sum(jnp.where(row == lane, span_ref[0:1, :], 0), axis=1, keepdims=True)
    end = jnp.sum(jnp.where(row == lane, span_ref[1:2, :], 0), axis=1, keepdims=True)
    inside = (begin <= lane) & (lane < end)
    o_ref[:, WIDTH:] = jnp.where((lane <= TILES) & ~inside, NEG, 0.0).astype(BF)


def prepare(queries, q_gain, spans):
    inputs = (queries, q_gain.reshape(1, HD), spans.T)
    return pl.pallas_call(
        prepare_kernel,
        grid=(1,),
        in_specs=[pl.BlockSpec(value.shape, lambda i: (0, 0)) for value in inputs],
        out_specs=pl.BlockSpec((ROWS, WIDTH + HD), lambda i: (0, 0)),
        out_shape=jax.ShapeDtypeStruct((ROWS, WIDTH + HD), BF),
        compiler_params=params(4),
        name="prepare",
    )(*(pltpu.with_memory_space_constraint(value, pltpu.HBM) for value in inputs))


def column(row, count):
    width = row.shape[1]
    across = lax.broadcasted_iota(jnp.int32, (count, width), 1)
    down = lax.broadcasted_iota(jnp.int32, (count, width), 0)
    return jnp.sum(jnp.where(across == down, row, 0.0), axis=1, keepdims=True)


def pack_kernel(place_ref, x_ref, own_ref, other_ref, gain_ref, o_ref):
    mean_sq = (column(own_ref[...], LOCAL) + column(other_ref[...], LOCAL)) / HD
    gain = gain_ref[...]
    gain = jnp.where(place_ref[0] == 0, gain, jnp.concatenate([gain[:, HD // 2 :]] * 2, axis=1))
    lane = lax.broadcasted_iota(jnp.int32, (LOCAL, HD), 1)
    field = x_ref[...]
    key = field / jnp.sqrt(mean_sq + EPSILON) * gain
    o_ref[...] = jnp.where(lane < HD // 2, key, field).astype(BF)


def pack(place, projected, own_squares, other_squares, k_gain):
    return pl.pallas_call(
        pack_kernel,
        in_specs=[smem(), vmem(), vmem(), vmem(), vmem()],
        out_specs=vmem(),
        out_shape=jax.ShapeDtypeStruct((LOCAL, HD), BF),
        compiler_params=params(4),
        name="pack",
    )(
        place,
        projected,
        own_squares.reshape(1, LOCAL),
        other_squares.reshape(1, LOCAL),
        k_gain.reshape(1, HD),
    )


def attend_kernel(place_ref, q_ref, far_ref, mine_ref, theirs_ref, o_ref, key_s, value_s):
    core, ylo = place_ref[0], place_ref[1]
    half = HD // 2
    lane = lax.broadcasted_iota(jnp.int32, (LOCAL, HD), 1)
    item = lax.broadcasted_iota(jnp.int32, (LOCAL, HD), 0)
    for block in range(BLOCKS):
        rows = slice(block * LOCAL, (block + 1) * LOCAL)
        mine, theirs = mine_ref[block], theirs_ref[block]
        left = jnp.where(core == 0, mine, theirs)
        right = jnp.where(core == 0, theirs, mine)
        key_s[rows, :HD] = jnp.concatenate([left[:, :half], right[:, :half]], axis=1)
        value_s[rows, :HD] = jnp.concatenate([left[:, half:], right[:, half:]], axis=1)
        tile = 2 * ylo + block // 8
        absent = item + (block % 8) * LOCAL >= place_ref[2 + tile]
        key_s[rows, HD:] = jnp.where(
            (lane == tile) | ((lane == TILES) & absent), 1.0, 0.0
        ).astype(BF)
    value_s[:, HD:] = jnp.ones((SLOTS, HD), BF)
    query_ext = jnp.concatenate([q_ref[:, WIDTH:], far_ref[:, WIDTH:]], axis=0)
    wide = lax.broadcasted_iota(jnp.int32, (2 * ROWS, HD), 1)
    totals = jnp.zeros((2 * ROWS, HD), F32)
    for head in range(HEADS):
        columns = slice(head * HD, (head + 1) * HD)
        query = jnp.concatenate([q_ref[:, columns], far_ref[:, columns]], axis=0)
        scores = lax.dot_general(
            jnp.concatenate([query, query_ext], axis=1),
            key_s[...],
            (((1,), (1,)), ((), ())),
            preferred_element_type=F32,
        )
        weights = jnp.exp2(scores * (math.log2(math.e) / math.sqrt(HD))).astype(BF)
        result = jnp.dot(weights, value_s[...], preferred_element_type=F32)
        numer = result[:, :HD].astype(BF)
        o_ref[ylo, :, columns] = numer[:ROWS]
        o_ref[1 - ylo, :, columns] = numer[ROWS:]
        totals = jnp.where(wide % HEADS == head, result[:, HD:], totals)
    high = totals.astype(BF)
    low = (totals - high.astype(F32)).astype(BF)
    packed = jnp.where(wide < HEADS, high.astype(F32), low.astype(F32)).astype(BF)
    o_ref[ylo, :, WIDTH:] = packed[:ROWS]
    o_ref[1 - ylo, :, WIDTH:] = packed[ROWS:]


def attend(place, query, far, mine, theirs):
    return pl.pallas_call(
        attend_kernel,
        in_specs=[smem(), vmem(), vmem(), vmem(), vmem()],
        out_specs=vmem(),
        out_shape=jax.ShapeDtypeStruct((2, ROWS, WIDTH + HD), BF),
        scratch_shapes=[pltpu.VMEM((SLOTS, 2 * HD), BF), pltpu.VMEM((SLOTS, 2 * HD), BF)],
        compiler_params=params(32),
        name="attend",
    )(place, query, far, mine, theirs)


def combine_kernel(near_ref, far_ref, o_ref):
    for block in range(2):
        summed = near_ref[block].astype(F32) + far_ref[block].astype(F32)
        for head in range(HEADS):
            columns = slice(head * HD, (head + 1) * HD)
            high = summed[:, WIDTH + head : WIDTH + head + 1]
            low = summed[:, WIDTH + HEADS + head : WIDTH + HEADS + head + 1]
            rows = slice(block * ROWS, (block + 1) * ROWS)
            o_ref[rows, columns] = (summed[:, columns] / (high + low)).astype(BF)


def combine(near, far):
    return pl.pallas_call(
        combine_kernel,
        in_specs=[vmem(), vmem()],
        out_specs=vmem(),
        out_shape=jax.ShapeDtypeStruct((2 * ROWS, WIDTH), BF),
        compiler_params=params(4),
        name="combine",
    )(near, far)


def project_kernel(place_ref, own_ref, other_hbm, w_hbm, o_ref, a_s, w_s, sem):
    steps = BLOCKS // 4
    other = pltpu.make_async_copy(other_hbm, a_s.at[:, pl.ds(WIDTH, WIDTH)], sem.at[steps])
    other.start()
    for step in range(steps):
        blocks = pl.ds(4 * step, 4)
        pltpu.make_async_copy(w_hbm.at[blocks], w_s.at[blocks], sem.at[step]).start()
    a_s[:, :WIDTH] = own_ref[...]
    other.wait()
    ylo = place_ref[1]

    def body(step, carry):
        blocks = pl.ds(4 * step, 4)
        pltpu.make_async_copy(w_hbm.at[blocks], w_s.at[blocks], sem.at[step]).wait()
        for index in range(2):
            block = 4 * step + 2 * index
            weight = jnp.concatenate([w_s[block], w_s[block + 1]], axis=1)
            result = jnp.dot(a_s[...], weight, preferred_element_type=F32).astype(BF)
            group = 2 * step + index
            o_ref[0, (group + 4 * ylo) & 7] = result[:ROWS]
            o_ref[1, (group + 4 - 4 * ylo) & 7] = result[ROWS:]
        return carry

    lax.fori_loop(0, steps, body, 0)


def project(place, own, other, weight):
    hbm = pl.BlockSpec(memory_space=pltpu.HBM)
    return pl.pallas_call(
        project_kernel,
        in_specs=[smem(), vmem(), hbm, hbm],
        out_specs=vmem(),
        out_shape=jax.ShapeDtypeStruct((2, 8, ROWS, 2 * HD), BF),
        scratch_shapes=[
            pltpu.VMEM((2 * ROWS, 2 * WIDTH), BF),
            pltpu.VMEM((BLOCKS, 2 * WIDTH, HD), BF),
            pltpu.SemaphoreType.DMA((5,)),
        ],
        compiler_params=params(12),
        name="project",
    )(
        place,
        own,
        pltpu.with_memory_space_constraint(other, pltpu.HBM),
        pltpu.with_memory_space_constraint(weight, pltpu.HBM),
    )


def reduce_kernel(x_ref, o_ref):
    for core in range(2):
        total = x_ref[core].astype(F32)
        for source in range(1, 8):
            total = total + x_ref[2 * source + core].astype(F32)
        total = total.astype(BF)
        o_ref[:, core * HD : (core + 1) * HD] = total[:, :HD]
        o_ref[:, (2 + core) * HD : (3 + core) * HD] = total[:, HD:]


def reduce(parts):
    return pl.pallas_call(
        reduce_kernel,
        in_specs=[vmem()],
        out_specs=vmem(),
        out_shape=jax.ShapeDtypeStruct((ROWS, WIDTH), BF),
        compiler_params=params(4),
        name="reduce",
    )(parts)


def local(queries, vision, kv_weight, out_weight, q_gain, k_gain, tile_counts, spans):
    core = lax.axis_index("core")
    ylo = lax.axis_index("ylo")
    half = HD // 2

    place = jnp.concatenate([jnp.stack([core, ylo]).astype(jnp.int32), tile_counts])

    query = prepare(queries, q_gain, spans)

    kept = lax.dynamic_slice_in_dim(out_weight, core * HD, HD, axis=1)
    sent = lax.dynamic_slice_in_dim(out_weight, (1 - core) * HD, HD, axis=1)
    got, query = lax.optimization_barrier((swapped(sent, "core"), query))
    pair = jnp.concatenate([kept, got], axis=0)
    far = swapped(query, "ylo")
    weight = lax.all_gather(pair, "z", axis=0, tiled=False)

    both = jnp.transpose(kv_weight, (0, 2, 1)).reshape(HD, vision.shape[1])
    projected = lax.dot_general(
        vision, both, (((1,), (1,)), ((), ())), preferred_element_type=F32
    )
    projected, far = lax.optimization_barrier((projected, far))
    key_raw = projected[:, :half]
    own_squares = jnp.sum(key_raw * key_raw, axis=1)
    local_pair = pack(place, projected, own_squares, swapped(own_squares, "core"), k_gain)
    mine = lax.all_gather(local_pair, "z", axis=0, tiled=False)
    theirs = swapped(mine, "core")

    partial = attend(place, query, far, mine, theirs)
    own = combine(partial, swapped(partial, "ylo"))
    other = swapped(own, "core")

    product = project(place, own, other, weight).reshape(16, ROWS, 2 * HD)
    parts = lax.all_to_all(product, ("x", "yhi", "core"), 0, 0, tiled=True)
    return placed(reduce(parts))


def solution(mesh):
    split = Mesh(mesh.devices.reshape(SIZES), AXES)
    seq, head = ("ylo", "z"), ("x", "yhi", "core")
    return jax.shard_map(
        local,
        mesh=split,
        in_specs=(
            P(seq, head),
            P(seq, None),
            P(None, None, head),
            P(head, seq),
            P(),
            P(),
            P(),
            P(seq, None),
        ),
        out_specs=P(seq, head),
        check_vma=False,
    )
```

```python
import math

import jax
import jax.numpy as jnp
from jax import lax
from jax.experimental import pallas as pl
from jax.experimental.pallas import tpu as pltpu
from jax.sharding import Mesh, PartitionSpec as P

HD = 128
TILES = 4
EPSILON = 1e-05
NEG = -1e30
AXES = ("ylo", "z", "x", "yhi", "core")
SIZES = (2, 16, 4, 2, 2)
ROWS = 128
HEADS = 4
WIDTH = HEADS * HD
LOCAL = 200
BLOCKS = 16
SLOTS = BLOCKS * LOCAL
BF = jnp.bfloat16
F32 = jnp.float32


def flat(ylo, z, x, yhi, core):
    return (((ylo * 16 + z) * 4 + x) * 2 + yhi) * 2 + core


def swapped(value, axis):
    return lax.ppermute(value, axis, [(0, 1), (1, 0)])


def placed(value):
    pairs = []
    for source in range(512):
        core, yhi, x, z = source % 2, source // 2 % 2, source // 4 % 4, source // 16 % 16
        ylo = source // 256
        stays = x // 2 == ylo
        target = source if stays else flat(1 - ylo, z, 3 - x, yhi, core)
        pairs.append((source, target))
    return lax.ppermute(value, AXES, pairs)


def vmem():
    return pl.BlockSpec(memory_space=pltpu.VMEM)


def smem():
    return pl.BlockSpec(memory_space=pltpu.SMEM)


def params(mib):
    return pltpu.CompilerParams(vmem_limit_bytes=mib << 20)


def prepare_kernel(q_ref, gain_ref, span_ref, o_ref):
    gain = gain_ref[...]
    for head in range(HEADS):
        columns = slice(head * HD, (head + 1) * HD)
        field = q_ref[:, columns].astype(F32)
        mean_sq = jnp.mean(field * field, axis=1, keepdims=True)
        o_ref[:, columns] = (field / jnp.sqrt(mean_sq + EPSILON) * gain).astype(BF)
    row = lax.broadcasted_iota(jnp.int32, (ROWS, HD), 0)
    lane = lax.broadcasted_iota(jnp.int32, (ROWS, HD), 1)
    begin = jnp.sum(jnp.where(row == lane, span_ref[0:1, :], 0), axis=1, keepdims=True)
    end = jnp.sum(jnp.where(row == lane, span_ref[1:2, :], 0), axis=1, keepdims=True)
    inside = (begin <= lane) & (lane < end)
    o_ref[:, WIDTH:] = jnp.where((lane <= TILES) & ~inside, NEG, 0.0).astype(BF)


def prepare(queries, q_gain, spans):
    inputs = (queries, q_gain.reshape(1, HD), spans.T)
    return pl.pallas_call(
        prepare_kernel,
        grid=(1,),
        in_specs=[pl.BlockSpec(value.shape, lambda i: (0, 0)) for value in inputs],
        out_specs=pl.BlockSpec((ROWS, WIDTH + HD), lambda i: (0, 0)),
        out_shape=jax.ShapeDtypeStruct((ROWS, WIDTH + HD), BF),
        compiler_params=params(4),
        name="prepare",
    )(*(pltpu.with_memory_space_constraint(value, pltpu.HBM) for value in inputs))


def column(row, count):
    width = row.shape[1]
    across = lax.broadcasted_iota(jnp.int32, (count, width), 1)
    down = lax.broadcasted_iota(jnp.int32, (count, width), 0)
    return jnp.sum(jnp.where(across == down, row, 0.0), axis=1, keepdims=True)


def pack_kernel(place_ref, x_ref, own_ref, other_ref, gain_ref, o_ref):
    mean_sq = (column(own_ref[...], LOCAL) + column(other_ref[...], LOCAL)) / HD
    gain = gain_ref[...]
    gain = jnp.where(place_ref[0] == 0, gain, jnp.concatenate([gain[:, HD // 2 :]] * 2, axis=1))
    lane = lax.broadcasted_iota(jnp.int32, (LOCAL, HD), 1)
    field = x_ref[...]
    key = field / jnp.sqrt(mean_sq + EPSILON) * gain
    o_ref[...] = jnp.where(lane < HD // 2, key, field).astype(BF)


def pack(place, projected, own_squares, other_squares, k_gain):
    return pl.pallas_call(
        pack_kernel,
        in_specs=[smem(), vmem(), vmem(), vmem(), vmem()],
        out_specs=vmem(),
        out_shape=jax.ShapeDtypeStruct((LOCAL, HD), BF),
        compiler_params=params(4),
        name="pack",
    )(
        place,
        projected,
        own_squares.reshape(1, LOCAL),
        other_squares.reshape(1, LOCAL),
        k_gain.reshape(1, HD),
    )


def attend_kernel(place_ref, q_ref, far_ref, mine_ref, theirs_ref, o_ref, key_s, value_s):
    core, ylo = place_ref[0], place_ref[1]
    half = HD // 2
    lane = lax.broadcasted_iota(jnp.int32, (LOCAL, HD), 1)
    item = lax.broadcasted_iota(jnp.int32, (LOCAL, HD), 0)
    for block in range(BLOCKS):
        rows = slice(block * LOCAL, (block + 1) * LOCAL)
        mine, theirs = mine_ref[block], theirs_ref[block]
        left = jnp.where(core == 0, mine, theirs)
        right = jnp.where(core == 0, theirs, mine)
        key_s[rows, :HD] = jnp.concatenate([left[:, :half], right[:, :half]], axis=1)
        value_s[rows, :HD] = jnp.concatenate([left[:, half:], right[:, half:]], axis=1)
        tile = 2 * ylo + block // 8
        absent = item + (block % 8) * LOCAL >= place_ref[2 + tile]
        key_s[rows, HD:] = jnp.where(
            (lane == tile) | ((lane == TILES) & absent), 1.0, 0.0
        ).astype(BF)
    value_s[:, HD:] = jnp.ones((SLOTS, HD), BF)
    query_ext = jnp.concatenate([q_ref[:, WIDTH:], far_ref[:, WIDTH:]], axis=0)
    wide = lax.broadcasted_iota(jnp.int32, (2 * ROWS, HD), 1)
    totals = jnp.zeros((2 * ROWS, HD), F32)
    for head in range(HEADS):
        columns = slice(head * HD, (head + 1) * HD)
        query = jnp.concatenate([q_ref[:, columns], far_ref[:, columns]], axis=0)
        scores = lax.dot_general(
            jnp.concatenate([query, query_ext], axis=1),
            key_s[...],
            (((1,), (1,)), ((), ())),
            preferred_element_type=F32,
        )
        weights = jnp.exp2(scores * (math.log2(math.e) / math.sqrt(HD))).astype(BF)
        result = jnp.dot(weights, value_s[...], preferred_element_type=F32)
        numer = result[:, :HD].astype(BF)
        o_ref[ylo, :, columns] = numer[:ROWS]
        o_ref[1 - ylo, :, columns] = numer[ROWS:]
        totals = jnp.where(wide % HEADS == head, result[:, HD:], totals)
    high = totals.astype(BF)
    low = (totals - high.astype(F32)).astype(BF)
    packed = jnp.where(wide < HEADS, high.astype(F32), low.astype(F32)).astype(BF)
    o_ref[ylo, :, WIDTH:] = packed[:ROWS]
    o_ref[1 - ylo, :, WIDTH:] = packed[ROWS:]


def attend(place, query, far, mine, theirs):
    return pl.pallas_call(
        attend_kernel,
        in_specs=[smem(), vmem(), vmem(), vmem(), vmem()],
        out_specs=vmem(),
        out_shape=jax.ShapeDtypeStruct((2, ROWS, WIDTH + HD), BF),
        scratch_shapes=[pltpu.VMEM((SLOTS, 2 * HD), BF), pltpu.VMEM((SLOTS, 2 * HD), BF)],
        compiler_params=params(32),
        name="attend",
    )(place, query, far, mine, theirs)


def combine_kernel(near_ref, far_ref, o_ref):
    for block in range(2):
        summed = near_ref[block].astype(F32) + far_ref[block].astype(F32)
        for head in range(HEADS):
            columns = slice(head * HD, (head + 1) * HD)
            high = summed[:, WIDTH + head : WIDTH + head + 1]
            low = summed[:, WIDTH + HEADS + head : WIDTH + HEADS + head + 1]
            rows = slice(block * ROWS, (block + 1) * ROWS)
            o_ref[rows, columns] = (summed[:, columns] / (high + low)).astype(BF)


def combine(near, far):
    return pl.pallas_call(
        combine_kernel,
        in_specs=[vmem(), vmem()],
        out_specs=vmem(),
        out_shape=jax.ShapeDtypeStruct((2 * ROWS, WIDTH), BF),
        compiler_params=params(4),
        name="combine",
    )(near, far)


def project_kernel(place_ref, own_ref, other_hbm, w_hbm, o_ref, a_s, w_s, sem):
    steps = BLOCKS // 4
    other = pltpu.make_async_copy(other_hbm, a_s.at[:, pl.ds(WIDTH, WIDTH)], sem.at[steps])
    other.start()
    for step in range(steps):
        blocks = pl.ds(4 * step, 4)
        pltpu.make_async_copy(w_hbm.at[blocks], w_s.at[blocks], sem.at[step]).start()
    a_s[:, :WIDTH] = own_ref[...]
    other.wait()
    ylo = place_ref[1]

    def body(step, carry):
        blocks = pl.ds(4 * step, 4)
        pltpu.make_async_copy(w_hbm.at[blocks], w_s.at[blocks], sem.at[step]).wait()
        for index in range(2):
            block = 4 * step + 2 * index
            weight = jnp.concatenate([w_s[block], w_s[block + 1]], axis=1)
            result = jnp.dot(a_s[...], weight, preferred_element_type=F32).astype(BF)
            group = 2 * step + index
            o_ref[0, (group + 4 * ylo) & 7] = result[:ROWS]
            o_ref[1, (group + 4 - 4 * ylo) & 7] = result[ROWS:]
        return carry

    lax.fori_loop(0, steps, body, 0)


def project(place, own, other, weight):
    hbm = pl.BlockSpec(memory_space=pltpu.HBM)
    return pl.pallas_call(
        project_kernel,
        in_specs=[smem(), vmem(), hbm, hbm],
        out_specs=vmem(),
        out_shape=jax.ShapeDtypeStruct((2, 8, ROWS, 2 * HD), BF),
        scratch_shapes=[
            pltpu.VMEM((2 * ROWS, 2 * WIDTH), BF),
            pltpu.VMEM((BLOCKS, 2 * WIDTH, HD), BF),
            pltpu.SemaphoreType.DMA((5,)),
        ],
        compiler_params=params(12),
        name="project",
    )(
        place,
        own,
        pltpu.with_memory_space_constraint(other, pltpu.HBM),
        pltpu.with_memory_space_constraint(weight, pltpu.HBM),
    )


def reduce_kernel(x_ref, o_ref):
    for core in range(2):
        total = x_ref[core].astype(F32)
        for source in range(1, 8):
            total = total + x_ref[2 * source + core].astype(F32)
        total = total.astype(BF)
        o_ref[:, core * HD : (core + 1) * HD] = total[:, :HD]
        o_ref[:, (2 + core) * HD : (3 + core) * HD] = total[:, HD:]


def reduce(parts):
    return pl.pallas_call(
        reduce_kernel,
        in_specs=[vmem()],
        out_specs=vmem(),
        out_shape=jax.ShapeDtypeStruct((ROWS, WIDTH), BF),
        compiler_params=params(4),
        name="reduce",
    )(parts)


def local(queries, vision, kv_weight, out_weight, q_gain, k_gain, tile_counts, spans):
    core = lax.axis_index("core")
    ylo = lax.axis_index("ylo")
    half = HD // 2

    place = jnp.concatenate([jnp.stack([core, ylo]).astype(jnp.int32), tile_counts])

    sent = lax.dynamic_slice_in_dim(out_weight, (1 - core) * HD, HD, axis=1)
    sent, out_weight = lax.optimization_barrier((sent, out_weight))
    kept = lax.dynamic_slice_in_dim(out_weight, core * HD, HD, axis=1)
    kept, got = lax.optimization_barrier((kept, swapped(sent, "core")))
    pair = jnp.concatenate([kept, got], axis=0)
    pair, queries = lax.optimization_barrier((pair, queries))
    query = prepare(queries, q_gain, spans)
    far = swapped(query, "ylo")
    weight = lax.all_gather(pair, "z", axis=0, tiled=False)

    both = jnp.transpose(kv_weight, (0, 2, 1)).reshape(HD, vision.shape[1])
    projected = lax.dot_general(
        vision, both, (((1,), (1,)), ((), ())), preferred_element_type=F32
    )
    projected, far = lax.optimization_barrier((projected, far))
    key_raw = projected[:, :half]
    own_squares = jnp.sum(key_raw * key_raw, axis=1)
    local_pair = pack(place, projected, own_squares, swapped(own_squares, "core"), k_gain)
    mine = lax.all_gather(local_pair, "z", axis=0, tiled=False)
    theirs = swapped(mine, "core")

    partial = attend(place, query, far, mine, theirs)
    own = combine(partial, swapped(partial, "ylo"))
    other = swapped(own, "core")

    product = project(place, own, other, weight).reshape(16, ROWS, 2 * HD)
    parts = lax.all_to_all(product, ("x", "yhi", "core"), 0, 0, tiled=True)
    return placed(reduce(parts))


def solution(mesh):
    split = Mesh(mesh.devices.reshape(SIZES), AXES)
    seq, head = ("ylo", "z"), ("x", "yhi", "core")
    return jax.shard_map(
        local,
        mesh=split,
        in_specs=(
            P(seq, head),
            P(seq, None),
            P(None, None, head),
            P(head, seq),
            P(),
            P(),
            P(),
            P(seq, None),
        ),
        out_specs=P(seq, head),
        check_vma=False,
    )
```
